256 devices in a mesh: row: 2 (over core), col: 8 (over z), layer: 16 (over y, x).
Axes of the slice: x: 4, y: 4, z: 8, core: 2. Of those that a mesh axis runs over, the one named last changes fastest.
Arguments:
- panel_top: float32 [16, 1024, 1024], P('layer', 'row', 'col'), as said below
- panel_win: float32 [16, 2048, 1024], P('layer', 'col', 'row'), may hold values from -0.375 to 0.375
- panel_rest: float32 [16, 2688, 1024], P('layer', 'row', 'col'), may hold values from -0.375 to 0.375
- trail_rest: float32 [16, 2688, 2048], P('layer', 'row', 'col'), may hold values from -2 to 2
Outputs:
- factor_top: float32 [1024, 1024], P('row', 'col')
- factor_win: float32 [2048, 1024], P('col', 'row')
- factor_rest: float32 [2688, 1024], P(('row', 'layer'), 'col')
- schur: float32 [2688, 2048], P(('row', 'layer'), 'col')
The draws below stay inside these ranges and needn't reach their ends.
Inputs may be any that keep to these rules, and one draw needn't show every extreme that they name: `panel_top`: each layer's block is symmetric, and the sum over the layers is positive definite with no eigenvalue under 0.25.
All inputs are finite; a program needn't handle non-finite values.
Results may differ from the reference program's by a relative error of at most 0.00021.
Values sent between devices are 32-bit elements; how exact they have to be, the bound alone decides.
No kernel may reach another device: no remote copies, remote signals or barrier semaphores. Data moves between devices by JAX's collectives and lax.ppermute only.
A program may use at most 128 MiB of HBM per device.

```python
import jax
import jax.numpy as jnp
from jax import lax

PW = 1024
W = 2048
REST = 2688
N_LAYER = 16


def draw_panel_top(key, part):
    columns_each = max(PW // (2 * N_LAYER), 1)
    base = jax.random.normal(jax.random.fold_in(key, 11), (N_LAYER, PW, columns_each), jnp.float32)
    gram = jnp.einsum('lik,ljk->lij', base, base, precision=lax.Precision.HIGHEST) * (2.75 / PW)
    shift = jax.random.uniform(jax.random.fold_in(key, 12), (N_LAYER, PW), jnp.float32, 0.25, 1.0) / N_LAYER
    identity = jnp.eye(PW, dtype=jnp.float32)
    return gram + shift[:, :, None] * identity[None, :, :]


def with_spikes(values, key, source, target, blocks, factor):
    owner, partner = [(jnp.arange(values.shape[dim]) // (values.shape[dim] // blocks)).reshape([-1 if axis == dim else 1 for axis in range(values.ndim)]) for dim in (source, target)]
    chosen = jax.random.permutation(key, blocks)[partner]
    strong = (owner == chosen) | (owner == (partner + blocks // 2) % blocks)
    return jnp.where(strong, factor * values, values)


def block_levels(rng, dims, cuts, least, high):
    level = 1.0
    for position, parts in cuts:
        steps = jax.random.uniform(jax.random.fold_in(jax.random.fold_in(rng, 6), position), (parts,), jnp.float32, least / len(cuts), high / len(cuts))
        level = level * jnp.repeat(jnp.exp(steps), dims[position] // parts).reshape((-1,) + (1,) * (len(dims) - 1 - position))
    return level


def scatter_about(own_key, dims, spread, reach, pieces=(), held_as=jnp.bfloat16):
    values = spread * jax.random.normal(own_key, dims, jnp.float32)
    if pieces:
        values = values * block_levels(own_key, dims, pieces, -0.22, 0.18)
    return jnp.clip(values, -reach, reach).astype(held_as)


def noise_with(rng, dims, width, limit, split, heavy, kind=jnp.bfloat16):
    array = width * jax.random.normal(rng, dims, jnp.float32)
    if split:
        array = array * block_levels(rng, dims, split, -0.22, 0.18)
    return jnp.clip(with_spikes(array, jax.random.fold_in(rng, 3), *heavy), -limit, limit).astype(kind)


def setup_inputs(seed: int = 0) -> dict:
    keys = jax.random.split(jax.random.key(seed), 5)
    panel_top = draw_panel_top(jax.random.fold_in(keys[4], 71), 0)
    panel_win = scatter_about(keys[1], (N_LAYER, W, PW), (16 * N_LAYER) ** -0.5, 0.375, ((0, 16), (1, 8), (2, 2)), jnp.float32)
    panel_rest = scatter_about(keys[2], (N_LAYER, REST, PW), (16 * N_LAYER) ** -0.5, 0.375, ((0, 16), (1, 2), (2, 8)), jnp.float32)
    trail_rest = noise_with(keys[3], (N_LAYER, REST, W), N_LAYER ** -0.5, 2.0, ((0, 16), (1, 2), (2, 8)), (0, 1, 16, 2.0), jnp.float32)
    return dict(panel_top=panel_top, panel_win=panel_win, panel_rest=panel_rest, trail_rest=trail_rest)


def solve_right(factor, values):
    return jax.scipy.linalg.solve_triangular(factor, values.T, lower=True).T

def reference(panel_top, panel_win, panel_rest, trail_rest):
    top_full = jnp.sum(panel_top, axis=0)
    window = jnp.sum(panel_win, axis=0)
    rest_sum = jnp.sum(panel_rest, axis=0)
    trail = jnp.sum(trail_rest, axis=0)
    factor_top = jnp.linalg.cholesky(top_full)
    factor_win = solve_right(factor_top, window)
    factor_rest = solve_right(factor_top, rest_sum)
    schur = trail - jnp.dot(factor_rest.astype(jnp.float32), factor_win.T.astype(jnp.float32), precision=lax.Precision.HIGHEST, preferred_element_type=jnp.float32)
    return (factor_top, factor_win, factor_rest, schur)
```

```python
import jax, jax.numpy as jnp
from jax import lax
from jax.sharding import PartitionSpec as P
from jax.experimental import pallas as pl
from jax.experimental.pallas import tpu as pltpu
HALF = 512
f32=jnp.float32; bf16=jnp.bfloat16
NN=(((1,),(0,)),((),())); NT=(((1,),(1,)),((),())); TN=(((0,),(0,)),((),()))

def split(a):
    hi=a.astype(bf16); lo=(a-hi.astype(f32)).astype(bf16)
    return hi,lo

def mm(a,b,dims=NN):
    ah,al=split(a); bh,bl=split(b)
    d=lambda x,y: lax.dot_general(x,y,dims,preferred_element_type=f32)
    return d(ah,bh)+(d(ah,bl)+d(al,bh))

def chol128(groups):
    lane=lax.broadcasted_iota(jnp.int32,(8,128),1)
    sub=lax.broadcasted_iota(jnp.int32,(8,128),0)
    bc=lambda x: jnp.broadcast_to(x,(8,128))
    S=list(groups); U=[]; W=[]
    for t in range(16):
        o=8*t
        St=S[t]
        inblk=(lane>=o)&(lane<o+8)
        P=[bc(St[i:i+1,:]) for i in range(8)]
        a=[[bc(P[i][:,o+j:o+j+1]) for j in range(i+1)] for i in range(8)]
        C={g:[bc(S[g][:,o+m:o+m+1]) for m in range(8)] for g in range(t+1,16)}
        P=[jnp.where(inblk,jnp.where(lane==o+i,1.0,0.0),P[i]) for i in range(8)]
        r=[None]*8; R=[None]*8
        for m in range(8):
            r[m]=lax.rsqrt(a[m][m])
            for i in range(m+1,8): a[i][m]=a[i][m]*r[m]
            a[m][m]=a[m][m]*r[m]
            for i in range(m+1,8):
                for j in range(m+1,i+1):
                    a[i][j]=a[i][j]-a[i][m]*a[j][m]
            R[m]=P[m]*r[m]
            for i in range(m+1,8): P[i]=P[i]-a[i][m]*R[m]
        V=[None]*8
        for m in range(7,-1,-1):
            acc=R[m]
            for j in range(7,m,-1): acc=acc-a[j][m]*V[j]
            V[m]=acc*r[m]
        for g in range(t+1,16):
            x=jnp.where(inblk,0.0,S[g])
            for m in range(8): x=x-C[g][m]*V[m]
            S[g]=x
        ut=jnp.zeros((8,128),f32); wt=ut
        for m in range(8):
            row=R[m]
            wt=jnp.where(sub==m,row,wt)
            for i in range(m,8): row=jnp.where(lane==o+i,a[i][m],row)
            if m: row=jnp.where((lane>=o)&(lane<o+m),0.0,row)
            ut=jnp.where(sub==m,row,ut)
        U.append(jnp.where(lane>=o,ut,0.0)); W.append(jnp.where(lane<o+8,wt,0.0))
    return U,W


def factor_loop(a_ref, u_ref, w_ref):
    n = a_ref.shape[0]

    def body(k, _):
        o = pl.multiple_of(k * 128, 128)
        rows = [pl.ds(pl.multiple_of(o + 8 * g, 8), 8) for g in range(16)]
        upper, inverse = chol128([a_ref[rows[g], pl.ds(o, 128)] for g in range(16)])
        for g in range(16):
            w_ref[k, 8 * g : 8 * g + 8, :] = inverse[g]
        panel = mm(w_ref[k], a_ref[pl.ds(o, 128), :])
        col = lax.broadcasted_iota(jnp.int32, (128, n), 1)
        panel = jnp.where(col >= o + 128, panel, 0.0)
        u_ref[pl.ds(o, 128), :] = panel
        for g in range(16):
            u_ref[rows[g], pl.ds(o, 128)] = upper[g]
        a_ref[...] = a_ref[...] - mm(panel, panel, TN)
        return 0

    lax.fori_loop(0, n // 128, body, 0)


def solve_half(x_ref, lanes, u_ref, w_ref):
    for k in range(HALF // 128):
        o = lanes + 128 * k
        value = x_ref[:, o : o + 128]
        if k:
            value = value - mm(x_ref[:, lanes:o], u_ref[0 : 128 * k, 128 * k : 128 * k + 128])
        x_ref[:, o : o + 128] = mm(value, w_ref[k], NT)


def place_strips(dst_ref, own_ref, other_ref, n_cols):
    q = lax.axis_index("row")
    for which, src in ((q, own_ref), (1 - q, other_ref)):
        for strip in range(src.shape[0]):
            start = pl.multiple_of(32 * strip + 16 * which, 16)
            for c in range(n_cols):
                dst_ref[pl.ds(start, 16), 128 * c : 128 * c + 128] = src[strip, c]


def first_kernel(own_ref, other_ref, u_ref, w_ref, a_ref):
    place_strips(a_ref, own_ref, other_ref, 4)
    factor_loop(a_ref, u_ref, w_ref)


def second_kernel(own_ref, other_ref, u1_ref, w1_ref, l21_ref, u_ref, w_ref, x_ref, a_ref):
    place_strips(x_ref, own_ref, other_ref, 8)
    solve_half(x_ref, 0, u1_ref, w1_ref)
    l21 = x_ref[:, :HALF]
    l21_ref[...] = l21
    a_ref[...] = x_ref[:, HALF:] - mm(l21, l21, NT)
    factor_loop(a_ref, u_ref, w_ref)


def third_kernel(
    own_ref, other_ref, rest_ref, trail_ref, u1_ref, w1_ref, l21_ref, u2_ref, w2_ref,
    top_out, win_out, rest_out, schur_out, x_ref,
):
    q = lax.axis_index("row")
    c = lax.axis_index("col")
    n_win = own_ref.shape[0]
    n_rest = rest_ref.shape[1]
    x_ref[n_win:, :] = jnp.zeros((x_ref.shape[0] - n_win, x_ref.shape[1]), f32)
    x_ref[0:n_win, pl.ds(pl.multiple_of(HALF * q, HALF), HALF)] = own_ref[...]
    x_ref[0:n_win, pl.ds(pl.multiple_of(HALF * (1 - q), HALF), HALF)] = other_ref[...]
    for j in range(rest_ref.shape[0]):
        x_ref[n_win : n_win + n_rest, 128 * j : 128 * j + 128] = rest_ref[j]
    solve_half(x_ref, 0, u1_ref, w1_ref)
    x_ref[:, HALF:] = x_ref[:, HALF:] - mm(x_ref[:, :HALF], l21_ref[...], NT)
    solve_half(x_ref, HALF, u2_ref, w2_ref)
    win_out[...] = x_ref[0:n_win, pl.ds(pl.multiple_of(HALF * q, HALF), HALF)]
    rest_out[...] = x_ref[n_win : n_win + n_rest, pl.ds(pl.multiple_of(128 * c, 128), 128)]
    product = mm(x_ref[n_win:, :], x_ref[0:n_win, :], NT)
    schur_out[...] = trail_ref[...] - product[0:n_rest]

    left = c < 4

    @pl.when(left & (q == 0))
    def _():
        top_out[...] = u1_ref[pl.ds(pl.multiple_of(128 * c, 128), 128), :].T

    @pl.when(jnp.logical_not(left) & (q == 0))
    def _():
        top_out[...] = jnp.zeros(top_out.shape, f32)

    @pl.when(left & (q == 1))
    def _():
        top_out[...] = l21_ref[:, pl.ds(pl.multiple_of(128 * c, 128), 128)]

    @pl.when(jnp.logical_not(left) & (q == 1))
    def _():
        top_out[...] = u2_ref[pl.ds(pl.multiple_of(128 * (c - 4), 128), 128), :].T


def call(kernel, outs, scratch, *args):
    shape = lambda s: jax.ShapeDtypeStruct(s, f32)
    return pl.pallas_call(
        kernel,
        out_shape=tuple(shape(s) for s in outs),
        scratch_shapes=[pltpu.VMEM(s, f32) for s in scratch],
        compiler_params=pltpu.CompilerParams(vmem_limit_bytes=48 << 20),
    )(*args)


def swap_rows(value):
    return lax.ppermute(value, "row", [(0, 1), (1, 0)])


def spread(value, axis):
    n = lax.axis_size(axis)
    return lax.all_to_all(jnp.broadcast_to(value, (n,) + value.shape), axis, 0, 0)


def reduce_pieces(value, axis):
    return lax.all_to_all(value, axis, 0, 0)


def per_device(panel_top, panel_win, panel_rest, trail_rest):
    top_parts = lax.all_to_all(panel_top[0].reshape(32, 16, 128), ("layer", "row"), 0, 0)
    top_piece = jnp.sum(top_parts.reshape(16, 2, 16, 128), axis=0)
    strips = spread(top_piece, "col")
    first_own = spread(strips[:4, 0], "layer")
    first_other = swap_rows(first_own)
    first_own, first_other, strips, panel_win, panel_rest, trail_rest = lax.optimization_barrier(
        (first_own, first_other, strips, panel_win, panel_rest, trail_rest)
    )
    second_own = spread(strips[:, 1], "layer")
    second_other = swap_rows(second_own)
    win_parts = lax.all_to_all(panel_win[0].reshape(16, 16, HALF), "layer", 0, 0)
    lower = jnp.concatenate(
        [panel_rest[0].reshape(16, 84, 128), trail_rest[0].reshape(16, 84, 256)], axis=2
    )
    lower_parts = lax.all_to_all(lower, "layer", 0, 0)
    u1, w1 = call(first_kernel, [(HALF, HALF), (4, 128, 128)], [(HALF, HALF)], first_own, first_other)
    win_own = spread(jnp.sum(win_parts, axis=0), "layer").reshape(256, HALF)
    win_other = swap_rows(win_own)
    lower_sum = jnp.sum(lower_parts, axis=0)
    rest_strips = spread(lower_sum[:, :128], "col")
    l21, u2, w2 = call(
        second_kernel,
        [(HALF, HALF), (HALF, HALF), (4, 128, 128)],
        [(HALF, 2 * HALF), (HALF, HALF)],
        second_own, second_other, u1, w1,
    )
    return call(
        third_kernel,
        [(HALF, 128), (256, HALF), (84, 128), (84, 256)],
        [(344, 2 * HALF)],
        win_own, win_other, rest_strips, lower_sum[:, 128:], u1, w1, l21, u2, w2,
    )


def solution(mesh):
    return jax.shard_map(
        per_device,
        mesh=mesh,
        in_specs=(
            P("layer", "row", "col"),
            P("layer", "col", "row"),
            P("layer", "row", "col"),
            P("layer", "row", "col"),
        ),
        out_specs=(
            P("row", "col"),
            P("col", "row"),
            P(("row", "layer"), "col"),
            P(("row", "layer"), "col"),
        ),
        check_vma=False,
    )
```

```python
import jax, jax.numpy as jnp
from jax import lax
from jax.sharding import PartitionSpec as P
from jax.experimental import pallas as pl
from jax.experimental.pallas import tpu as pltpu
HALF = 512
f32=jnp.float32; bf16=jnp.bfloat16
NN=(((1,),(0,)),((),())); NT=(((1,),(1,)),((),())); TN=(((0,),(0,)),((),()))

def split(a):
    hi=a.astype(bf16); lo=(a-hi.astype(f32)).astype(bf16)
    return hi,lo

def mm(a,b,dims=NN):
    ah,al=split(a); bh,bl=split(b)
    d=lambda x,y: lax.dot_general(x,y,dims,preferred_element_type=f32)
    return d(ah,bh)+(d(ah,bl)+d(al,bh))

def chol128(groups):
    lane=lax.broadcasted_iota(jnp.int32,(8,128),1)
    sub=lax.broadcasted_iota(jnp.int32,(8,128),0)
    bc=lambda x: jnp.broadcast_to(x,(8,128))
    S=list(groups); U=[]; W=[]
    for t in range(16):
        o=8*t
        St=S[t]
        inblk=(lane>=o)&(lane<o+8)
        P=[bc(St[i:i+1,:]) for i in range(8)]
        a=[[bc(P[i][:,o+j:o+j+1]) for j in range(i+1)] for i in range(8)]
        C={g:[bc(S[g][:,o+m:o+m+1]) for m in range(8)] for g in range(t+1,16)}
        P=[jnp.where(inblk,jnp.where(lane==o+i,1.0,0.0),P[i]) for i in range(8)]
        r=[None]*8; R=[None]*8
        for m in range(8):
            r[m]=lax.rsqrt(a[m][m])
            for i in range(m+1,8): a[i][m]=a[i][m]*r[m]
            a[m][m]=a[m][m]*r[m]
            for i in range(m+1,8):
                for j in range(m+1,i+1):
                    a[i][j]=a[i][j]-a[i][m]*a[j][m]
            R[m]=P[m]*r[m]
            for i in range(m+1,8): P[i]=P[i]-a[i][m]*R[m]
        V=[None]*8
        for m in range(7,-1,-1):
            acc=R[m]
            for j in range(7,m,-1): acc=acc-a[j][m]*V[j]
            V[m]=acc*r[m]
        for g in range(t+1,16):
            x=jnp.where(inblk,0.0,S[g])
            for m in range(8): x=x-C[g][m]*V[m]
            S[g]=x
        ut=jnp.zeros((8,128),f32); wt=ut
        for m in range(8):
            row=R[m]
            wt=jnp.where(sub==m,row,wt)
            for i in range(m,8): row=jnp.where(lane==o+i,a[i][m],row)
            if m: row=jnp.where((lane>=o)&(lane<o+m),0.0,row)
            ut=jnp.where(sub==m,row,ut)
        U.append(jnp.where(lane>=o,ut,0.0)); W.append(jnp.where(lane<o+8,wt,0.0))
    return U,W


def factor_loop(a_ref, u_ref, w_ref):
    n = a_ref.shape[0]

    def body(k, _):
        o = pl.multiple_of(k * 128, 128)
        rows = [pl.ds(pl.multiple_of(o + 8 * g, 8), 8) for g in range(16)]
        upper, inverse = chol128([a_ref[rows[g], pl.ds(o, 128)] for g in range(16)])
        for g in range(16):
            w_ref[k, 8 * g : 8 * g + 8, :] = inverse[g]
        panel = mm(w_ref[k], a_ref[pl.ds(o, 128), :])
        col = lax.broadcasted_iota(jnp.int32, (128, n), 1)
        panel = jnp.where(col >= o + 128, panel, 0.0)
        u_ref[pl.ds(o, 128), :] = panel
        for g in range(16):
            u_ref[rows[g], pl.ds(o, 128)] = upper[g]
        a_ref[...] = a_ref[...] - mm(panel, panel, TN)
        return 0

    lax.fori_loop(0, n // 128, body, 0)


def solve_half(x_ref, first, lanes, u_ref, w_ref):
    for k in range(HALF // 128):
        o = lanes + 128 * k
        value = x_ref[first:, o : o + 128]
        if k:
            value = value - mm(
                x_ref[first:, lanes:o], u_ref[0 : 128 * k, 128 * k : 128 * k + 128]
            )
        x_ref[first:, o : o + 128] = mm(value, w_ref[k], NT)


def aligned(index, step):
    return pl.ds(pl.multiple_of(index * step, step), step)


def pack_kernel(top_ref, win_ref, rest_ref, out_ref):
    for piece in range(out_ref.shape[0]):
        for j in range(4):
            out_ref[piece, 16 * j : 16 * j + 16] = win_ref[
                16 * piece : 16 * piece + 16, 128 * j : 128 * j + 128
            ]
        out_ref[piece, 64:96] = top_ref[32 * piece : 32 * piece + 32]
        out_ref[piece, 96:180] = rest_ref[84 * piece : 84 * piece + 84]


def first_kernel(own_ref, other_ref, u_ref, w_ref, a_ref):
    q = lax.axis_index("row")
    for which, src in ((q, own_ref), (1 - q, other_ref)):
        for strip in range(src.shape[0]):
            for c in range(4):
                a_ref[aligned(2 * strip + which, 16), 128 * c : 128 * c + 128] = src[
                    strip, 16 * c : 16 * c + 16
                ]
    factor_loop(a_ref, u_ref, w_ref)


def second_kernel(
    own_ref, other_ref, own2_ref, other2_ref, strips_ref, u1_ref, w1_ref,
    top_out, win_out, rest_out, product_out, u2_ref, w2_ref, x_ref, a_ref,
):
    q = lax.axis_index("row")
    c = lax.axis_index("col")
    n_win = win_out.shape[0]
    n_rest = rest_out.shape[0]
    win = HALF
    rest = HALF + n_win
    x_ref[rest:, :] = jnp.zeros((x_ref.shape[0] - rest, x_ref.shape[1]), f32)
    for which, top_src, win_src in ((q, own2_ref, own_ref), (1 - q, other2_ref, other_ref)):
        for strip in range(top_src.shape[0]):
            for j in range(8):
                x_ref[aligned(2 * strip + which, 16), 128 * j : 128 * j + 128] = top_src[strip, j]
            for j in range(4):
                x_ref[win + 16 * strip : win + 16 * strip + 16, aligned(4 * which + j, 128)] = (
                    win_src[strip, 64 + 16 * j : 80 + 16 * j]
                )
    for j in range(8):
        x_ref[rest : rest + n_rest, 128 * j : 128 * j + 128] = strips_ref[j, 32 : 32 + n_rest]
    solve_half(x_ref, 0, 0, u1_ref, w1_ref)
    x_ref[:, HALF:] = x_ref[:, HALF:] - mm(x_ref[:, :HALF], x_ref[:HALF, :HALF], NT)
    a_ref[...] = x_ref[:HALF, HALF:]
    factor_loop(a_ref, u2_ref, w2_ref)
    solve_half(x_ref, HALF, HALF, u2_ref, w2_ref)
    win_out[...] = x_ref[win:rest, aligned(q, HALF)]
    rest_out[...] = x_ref[rest : rest + n_rest, aligned(c, 128)]
    product_out[...] = mm(x_ref[rest:, :], x_ref[win:rest, :], NT)[0:n_rest]
    left = c < 4

    @pl.when(left & (q == 0))
    def _():
        top_out[...] = u1_ref[aligned(c, 128), :].T

    @pl.when(jnp.logical_not(left) & (q == 0))
    def _():
        top_out[...] = jnp.zeros(top_out.shape, f32)

    @pl.when(left & (q == 1))
    def _():
        top_out[...] = x_ref[:HALF, aligned(c, 128)]

    @pl.when(jnp.logical_not(left) & (q == 1))
    def _():
        top_out[...] = u2_ref[aligned(c - 4, 128), :].T


def call(kernel, outs, scratch, micros, *args):
    shape = lambda s: jax.ShapeDtypeStruct(s, f32)
    return pl.pallas_call(
        kernel,
        out_shape=tuple(shape(s) for s in outs),
        scratch_shapes=[pltpu.VMEM(s, f32) for s in scratch],
        compiler_params=pltpu.CompilerParams(vmem_limit_bytes=48 << 20),
        cost_estimate=pl.CostEstimate(
            flops=int(micros * 1e9), transcendentals=0, bytes_accessed=int(micros * 3e6)
        ),
    )(*args)


def swap_rows(value):
    return lax.ppermute(value, "row", [(0, 1), (1, 0)])


def spread(value, axis):
    n = lax.axis_size(axis)
    return lax.all_to_all(jnp.broadcast_to(value, (n,) + value.shape), axis, 0, 0)


def per_device(panel_top, panel_win, panel_rest, trail_rest):
    q = lax.axis_index("row")
    (pieces,) = call(pack_kernel, [(16, 180, 128)], [], 2, panel_top[0], panel_win[0], panel_rest[0])
    sums = jnp.sum(lax.all_to_all(pieces, "layer", 0, 0), axis=0)
    strips = spread(sums[64:], "col")
    kept = lax.dynamic_slice_in_dim(strips, 16 * q, 16, 1)
    got = swap_rows(lax.dynamic_slice_in_dim(strips, 16 * (1 - q), 16, 1))
    half0 = jnp.where(q == 0, kept[:4], got[:4])
    half1 = jnp.where(q == 0, got, kept)
    own = spread(jnp.concatenate([half0.reshape(64, 128), sums[:64]], axis=0), "layer")
    other = swap_rows(own)
    own, other, half1, trail_rest = lax.optimization_barrier((own, other, half1, trail_rest))
    own2 = spread(half1, "layer")
    u1, w1 = call(first_kernel, [(HALF, HALF), (4, 128, 128)], [(HALF, HALF)], 24, own, other)
    own2, u1, trail_rest = lax.optimization_barrier((own2, u1, trail_rest))
    other2 = swap_rows(own2)
    trail_parts = lax.all_to_all(trail_rest[0].reshape(16, 84, 256), "layer", 0, 0)
    top_block, win_block, rest_block, product = call(
        second_kernel,
        [(HALF, 128), (256, HALF), (84, 128), (84, 256)],
        [(HALF, HALF), (4, 128, 128), (856, 2 * HALF), (HALF, HALF)],
        30, own, other, own2, other2, strips, u1, w1,
    )
    return top_block, win_block, rest_block, jnp.sum(trail_parts, axis=0) - product


def solution(mesh):
    return jax.shard_map(
        per_device,
        mesh=mesh,
        in_specs=(
            P("layer", "row", "col"),
            P("layer", "col", "row"),
            P("layer", "row", "col"),
            P("layer", "row", "col"),
        ),
        out_specs=(
            P("row", "col"),
            P("col", "row"),
            P(("row", "layer"), "col"),
            P(("row", "layer"), "col"),
        ),
        check_vma=False,
    )
```

```python
import jax, jax.numpy as jnp
from jax import lax
from jax.sharding import PartitionSpec as P
from jax.experimental import pallas as pl
from jax.experimental.pallas import tpu as pltpu
HALF = 512
f32=jnp.float32; bf16=jnp.bfloat16
NN=(((1,),(0,)),((),())); NT=(((1,),(1,)),((),())); TN=(((0,),(0,)),((),()))

def split(a):
    hi=a.astype(bf16); lo=(a-hi.astype(f32)).astype(bf16)
    return hi,lo

def mm(a,b,dims=NN):
    ah,al=split(a); bh,bl=split(b)
    d=lambda x,y: lax.dot_general(x,y,dims,preferred_element_type=f32)
    return d(ah,bh)+(d(ah,bl)+d(al,bh))

def block_inverse(block):
    lane = lax.broadcasted_iota(jnp.int32, (8, 128), 1)
    sub = lax.broadcasted_iota(jnp.int32, (8, 128), 0)
    wide = lambda x: jnp.broadcast_to(x, (8, 128))
    S = [block[8 * g : 8 * g + 8] for g in range(16)]
    inverse = []
    for t in range(8):
        o = 16 * t
        inside = (lane >= o) & (lane < o + 16)
        mine = (2 * t, 2 * t + 1)
        cols = [[wide(S[g][:, o + j : o + j + 1]) for g in mine] for j in range(16)]
        P = [
            jnp.where(inside, jnp.where(lane - o - 8 * k == sub, 1.0, 0.0), S[g])
            for k, g in enumerate(mine)
        ]
        rows = [jnp.zeros((8, 128), f32)] * 2
        pivots = [jnp.ones((8, 128), f32)] * 2
        for m in range(16):
            k, s = divmod(m, 8)
            here = sub == s
            pivot = wide(cols[m][k][s : s + 1])
            scale = 1.0 / pivot
            pivots[k] = jnp.where(here, pivot, pivots[k])
            rows[k] = jnp.where(here, P[k], rows[k])
            for j in range(m + 1, 16):
                f = wide(cols[j][k][s : s + 1]) * scale
                for i in range(2):
                    x = cols[j][i] - cols[m][i] * f
                    cols[j][i] = jnp.where(here, f, x) if i == k else x
            f = wide(P[k][s : s + 1]) * scale
            for i in range(2):
                x = P[i] - cols[m][i] * f
                P[i] = jnp.where(here, f, x) if i == k else x
        V = [wide(P[m // 8][m % 8 : m % 8 + 1]) for m in range(16)]
        for g in range(2 * t + 2, min(16, 2 * t + 4)):
            x = jnp.where(inside, 0.0, S[g])
            for m in range(16):
                x = x - wide(S[g][:, o + m : o + m + 1]) * V[m]
            S[g] = x
        far = range(2 * t + 4, 16)
        if far:
            pads = [jnp.zeros((n, 128), bf16) for n in (o, 112 - o)]
            full = lambda v: jnp.concatenate(
                [x for x in (pads[0], v, pads[1]) if x.shape[0]], axis=0
            )
            vh, vl = (full(v) for v in split(jnp.concatenate(P, axis=0)))
            xh, xl = split(jnp.concatenate([S[g] for g in far], axis=0))
            d = lambda x, y: lax.dot_general(x, y, NN, preferred_element_type=f32)
            y = d(xh, vh) + (d(xh, vl) + d(xl, vh))
            for n, g in enumerate(far):
                S[g] = jnp.where(inside, 0.0, S[g]) - y[8 * n : 8 * n + 8]
        for k in range(2):
            inverse.append(jnp.where(lane < o + 16, rows[k] * lax.rsqrt(pivots[k]), 0.0))
    return jnp.concatenate(inverse, axis=0)


def factor_loop(a_ref, u_ref, w_ref):
    n = a_ref.shape[0]
    blocks = n // 128
    ahead = lax.broadcasted_iota(jnp.int32, (128, n), 1) - lax.broadcasted_iota(
        jnp.int32, (128, n), 0
    )

    def step(k, diagonal, first=False):
        o = pl.multiple_of(k * 128, 128)
        inverse = block_inverse(diagonal)
        if not first:
            past = u_ref[pl.ds(pl.multiple_of(k * 128 - 128, 128), 128), :]
            a_ref[...] = a_ref[...] - mm(past, past, TN)
        w_ref[k] = inverse
        panel = mm(inverse, a_ref[pl.ds(o, 128), :])
        u_ref[pl.ds(o, 128), :] = jnp.where(ahead >= o, panel, 0.0)
        following = pl.ds(pl.multiple_of(jnp.minimum(k + 1, blocks - 1) * 128, 128), 128)
        corner = u_ref[pl.ds(o, 128), following]
        return a_ref[following, following] - mm(corner, corner, TN)

    lax.fori_loop(1, blocks, step, step(0, a_ref[0:128, 0:128], True))


def solve_half(x_ref, first, lanes, u_ref, w_ref):
    for k in range(HALF // 128):
        o = lanes + 128 * k
        value = x_ref[first:, o : o + 128]
        if k:
            value = value - mm(
                x_ref[first:, lanes:o], u_ref[0 : 128 * k, 128 * k : 128 * k + 128]
            )
        x_ref[first:, o : o + 128] = mm(value, w_ref[k], NT)


def aligned(index, step):
    return pl.ds(pl.multiple_of(index * step, step), step)


def pack_kernel(top_ref, win_ref, rest_ref, out_ref):
    for piece in range(out_ref.shape[0]):
        for j in range(4):
            out_ref[piece, 16 * j : 16 * j + 16] = win_ref[
                16 * piece : 16 * piece + 16, 128 * j : 128 * j + 128
            ]
        out_ref[piece, 64:96] = top_ref[32 * piece : 32 * piece + 32]
        out_ref[piece, 96:180] = rest_ref[84 * piece : 84 * piece + 84]


def first_kernel(own_ref, other_ref, u_ref, w_ref, a_ref):
    q = lax.axis_index("row")
    for which, src in ((q, own_ref), (1 - q, other_ref)):
        for strip in range(src.shape[0]):
            for c in range(4):
                a_ref[aligned(2 * strip + which, 16), 128 * c : 128 * c + 128] = src[
                    strip, 16 * c : 16 * c + 16
                ]
    factor_loop(a_ref, u_ref, w_ref)


def second_kernel(
    own_ref, other_ref, own2_ref, other2_ref, strips_ref, u1_ref, w1_ref,
    top_out, win_out, rest_out, product_out, u2_ref, w2_ref, x_ref, a_ref,
):
    q = lax.axis_index("row")
    c = lax.axis_index("col")
    n_win = win_out.shape[0]
    n_rest = rest_out.shape[0]
    win = HALF
    rest = HALF + n_win
    x_ref[rest:, :] = jnp.zeros((x_ref.shape[0] - rest, x_ref.shape[1]), f32)
    for which, top_src, win_src in ((q, own2_ref, own_ref), (1 - q, other2_ref, other_ref)):
        for strip in range(top_src.shape[0]):
            for j in range(8):
                x_ref[aligned(2 * strip + which, 16), 128 * j : 128 * j + 128] = top_src[strip, j]
            for j in range(4):
                x_ref[win + 16 * strip : win + 16 * strip + 16, aligned(4 * which + j, 128)] = (
                    win_src[strip, 64 + 16 * j : 80 + 16 * j]
                )
    for j in range(8):
        x_ref[rest : rest + n_rest, 128 * j : 128 * j + 128] = strips_ref[j, 32 : 32 + n_rest]
    solve_half(x_ref, 0, 0, u1_ref, w1_ref)
    x_ref[:, HALF:] = x_ref[:, HALF:] - mm(x_ref[:, :HALF], x_ref[:HALF, :HALF], NT)
    a_ref[...] = x_ref[:HALF, HALF:]
    factor_loop(a_ref, u2_ref, w2_ref)
    solve_half(x_ref, HALF, HALF, u2_ref, w2_ref)
    win_out[...] = x_ref[win:rest, aligned(q, HALF)]
    rest_out[...] = x_ref[rest : rest + n_rest, aligned(c, 128)]
    product_out[...] = mm(x_ref[rest:, :], x_ref[win:rest, :], NT)[0:n_rest]
    left = c < 4

    @pl.when(left & (q == 0))
    def _():
        top_out[...] = u1_ref[aligned(c, 128), :].T

    @pl.when(jnp.logical_not(left) & (q == 0))
    def _():
        top_out[...] = jnp.zeros(top_out.shape, f32)

    @pl.when(left & (q == 1))
    def _():
        top_out[...] = x_ref[:HALF, aligned(c, 128)]

    @pl.when(jnp.logical_not(left) & (q == 1))
    def _():
        top_out[...] = u2_ref[aligned(c - 4, 128), :].T


def call(kernel, outs, scratch, micros, *args):
    shape = lambda s: jax.ShapeDtypeStruct(s, f32)
    return pl.pallas_call(
        kernel,
        out_shape=tuple(shape(s) for s in outs),
        scratch_shapes=[pltpu.VMEM(s, f32) for s in scratch],
        compiler_params=pltpu.CompilerParams(vmem_limit_bytes=48 << 20),
        cost_estimate=pl.CostEstimate(
            flops=int(micros * 1e9), transcendentals=0, bytes_accessed=int(micros * 3e6)
        ),
    )(*args)


def swap_rows(value):
    return lax.ppermute(value, "row", [(0, 1), (1, 0)])


def spread(value, axis):
    n = lax.axis_size(axis)
    return lax.all_to_all(jnp.broadcast_to(value, (n,) + value.shape), axis, 0, 0)


def per_device(panel_top, panel_win, panel_rest, trail_rest):
    q = lax.axis_index("row")
    (pieces,) = call(pack_kernel, [(16, 180, 128)], [], 2, panel_top[0], panel_win[0], panel_rest[0])
    sums = jnp.sum(lax.all_to_all(pieces, "layer", 0, 0), axis=0)
    strips = spread(sums[64:], "col")
    kept = lax.dynamic_slice_in_dim(strips, 16 * q, 16, 1)
    got = swap_rows(lax.dynamic_slice_in_dim(strips, 16 * (1 - q), 16, 1))
    half0 = jnp.where(q == 0, kept[:4], got[:4])
    half1 = jnp.where(q == 0, got, kept)
    own = spread(jnp.concatenate([half0.reshape(64, 128), sums[:64]], axis=0), "layer")
    other = swap_rows(own)
    own, other, half1, trail_rest = lax.optimization_barrier((own, other, half1, trail_rest))
    own2 = spread(half1, "layer")
    u1, w1 = call(first_kernel, [(HALF, HALF), (4, 128, 128)], [(HALF, HALF)], 24, own, other)
    own2, u1, trail_rest = lax.optimization_barrier((own2, u1, trail_rest))
    other2 = swap_rows(own2)
    trail_parts = lax.all_to_all(trail_rest[0].reshape(16, 84, 256), "layer", 0, 0)
    top_block, win_block, rest_block, product = call(
        second_kernel,
        [(HALF, 128), (256, HALF), (84, 128), (84, 256)],
        [(HALF, HALF), (4, 128, 128), (856, 2 * HALF), (HALF, HALF)],
        30, own, other, own2, other2, strips, u1, w1,
    )
    return top_block, win_block, rest_block, jnp.sum(trail_parts, axis=0) - product


def solution(mesh):
    return jax.shard_map(
        per_device,
        mesh=mesh,
        in_specs=(
            P("layer", "row", "col"),
            P("layer", "col", "row"),
            P("layer", "row", "col"),
            P("layer", "row", "col"),
        ),
        out_specs=(
            P("row", "col"),
            P("col", "row"),
            P(("row", "layer"), "col"),
            P(("row", "layer"), "col"),
        ),
        check_vma=False,
    )
```

```python
import jax, jax.numpy as jnp
from jax import lax
from jax.sharding import PartitionSpec as P
from jax.experimental import pallas as pl
from jax.experimental.pallas import tpu as pltpu
HALF = 512
f32=jnp.float32; bf16=jnp.bfloat16
NN=(((1,),(0,)),((),())); NT=(((1,),(1,)),((),())); TN=(((0,),(0,)),((),()))

def split(a):
    hi=a.astype(bf16); lo=(a-hi.astype(f32)).astype(bf16)
    return hi,lo

def mm(a,b,dims=NN):
    ah,al=split(a); bh,bl=split(b)
    d=lambda x,y: lax.dot_general(x,y,dims,preferred_element_type=f32)
    return d(ah,bh)+(d(ah,bl)+d(al,bh))

def block_inverse(block):
    lane = lax.broadcasted_iota(jnp.int32, (8, 128), 1)
    sub = lax.broadcasted_iota(jnp.int32, (8, 128), 0)
    wide = lambda x: jnp.broadcast_to(x, (8, 128))
    S = [block[8 * g : 8 * g + 8] for g in range(16)]
    inverse = []
    for t in range(8):
        o = 16 * t
        inside = (lane >= o) & (lane < o + 16)
        mine = (2 * t, 2 * t + 1)
        cols = [[wide(S[g][:, o + j : o + j + 1]) for g in mine] for j in range(16)]
        P = [
            jnp.where(inside, jnp.where(lane - o - 8 * k == sub, 1.0, 0.0), S[g])
            for k, g in enumerate(mine)
        ]
        rows = [jnp.zeros((8, 128), f32)] * 2
        pivots = [jnp.ones((8, 128), f32)] * 2
        for m in range(16):
            k, s = divmod(m, 8)
            here = sub == s
            pivot = wide(cols[m][k][s : s + 1])
            scale = 1.0 / pivot
            pivots[k] = jnp.where(here, pivot, pivots[k])
            rows[k] = jnp.where(here, P[k], rows[k])
            for j in range(m + 1, 16):
                f = wide(cols[j][k][s : s + 1]) * scale
                for i in range(2):
                    x = cols[j][i] - cols[m][i] * f
                    cols[j][i] = jnp.where(here, f, x) if i == k else x
            f = wide(P[k][s : s + 1]) * scale
            for i in range(2):
                x = P[i] - cols[m][i] * f
                P[i] = jnp.where(here, f, x) if i == k else x
        V = [wide(P[m // 8][m % 8 : m % 8 + 1]) for m in range(16)]
        for g in range(2 * t + 2, min(16, 2 * t + 4)):
            x = jnp.where(inside, 0.0, S[g])
            for m in range(16):
                x = x - wide(S[g][:, o + m : o + m + 1]) * V[m]
            S[g] = x
        far = range(2 * t + 4, 16)
        if far:
            pads = [jnp.zeros((n, 128), bf16) for n in (o, 112 - o)]
            full = lambda v: jnp.concatenate(
                [x for x in (pads[0], v, pads[1]) if x.shape[0]], axis=0
            )
            vh, vl = (full(v) for v in split(jnp.concatenate(P, axis=0)))
            xh, xl = split(jnp.concatenate([S[g] for g in far], axis=0))
            d = lambda x, y: lax.dot_general(x, y, NN, preferred_element_type=f32)
            y = d(xh, vh) + (d(xh, vl) + d(xl, vh))
            for n, g in enumerate(far):
                S[g] = jnp.where(inside, 0.0, S[g]) - y[8 * n : 8 * n + 8]
        for k in range(2):
            inverse.append(jnp.where(lane < o + 16, rows[k] * lax.rsqrt(pivots[k]), 0.0))
    return jnp.concatenate(inverse, axis=0)


def factor_loop(a_ref, u_ref, w_ref, b_ref, beside=lambda: None):
    n = a_ref.shape[0]
    blocks = n // 128
    ahead = lax.broadcasted_iota(jnp.int32, (128, n), 1) - lax.broadcasted_iota(
        jnp.int32, (128, n), 0
    )

    def solve(k):
        here = pl.ds(pl.multiple_of(k * 128, 128), 128)
        return here, mm(b_ref[:, here], w_ref[k], NT)

    def step(k, diagonal, first=False):
        o = pl.multiple_of(k * 128, 128)
        inverse = block_inverse(diagonal)
        if first:
            beside()
        else:
            past = u_ref[pl.ds(pl.multiple_of(k * 128 - 128, 128), 128), :]
            a_ref[...] = a_ref[...] - mm(past, past, TN)
            before, solved = solve(k - 1)
            b_ref[...] = b_ref[...] - mm(solved, past)
            b_ref[:, before] = solved
        w_ref[k] = inverse
        panel = mm(inverse, a_ref[pl.ds(o, 128), :])
        u_ref[pl.ds(o, 128), :] = jnp.where(ahead >= o, panel, 0.0)
        following = pl.ds(pl.multiple_of(jnp.minimum(k + 1, blocks - 1) * 128, 128), 128)
        corner = u_ref[pl.ds(o, 128), following]
        return a_ref[following, following] - mm(corner, corner, TN)

    lax.fori_loop(1, blocks, step, step(0, a_ref[0:128, 0:128], True))
    last, solved = solve(blocks - 1)
    b_ref[:, last] = solved


def solve_rows(x_ref, u_ref, w_ref):
    for k in range(x_ref.shape[1] // 128):
        here = slice(128 * k, 128 * k + 128)
        value = x_ref[:, here]
        if k:
            value = value - mm(x_ref[:, : 128 * k], u_ref[0 : 128 * k, here])
        x_ref[:, here] = mm(value, w_ref[k], NT)


def aligned(index, step):
    return pl.ds(pl.multiple_of(index * step, step), step)


def pack_kernel(top_ref, win_ref, rest_ref, out_ref, whole_ref, sems):
    moves = [
        (win_ref.at[:, :, 128 * j : 128 * j + 128], out_ref.at[:, 8 * j : 8 * j + 8])
        for j in range(4)
    ] + [(top_ref, out_ref.at[:, 32:48]), (rest_ref, whole_ref)]
    copies = [pltpu.make_async_copy(*move, sems.at[n]) for n, move in enumerate(moves)]
    for copy in copies[::-1]:
        copy.start()
    for copy in copies[::-1]:
        copy.wait()
    for piece in range(out_ref.shape[0]):
        out_ref[piece, 48:90] = whole_ref[42 * piece : 42 * piece + 42]


def place_top(q, own_ref, other_ref, refs):
    for which, src in ((q, own_ref), (1 - q, other_ref)):
        for strip in range(src.shape[0]):
            for n, dst in enumerate(refs):
                for c in range(4):
                    first = 64 * n + 16 * c
                    dst[aligned(2 * strip + which, 16), 128 * c : 128 * c + 128] = src[
                        strip, first : first + 16
                    ]


def place_lower(q, half, own_ref, other_ref, rest_own_ref, rest_other_ref, b_ref):
    win = 16 * own_ref.shape[0]
    for which, src in ((q, own_ref), (1 - q, other_ref)):
        for strip in range(src.shape[0]):
            for j in range(4):
                first = 64 + 32 * half + 8 * j
                b_ref[aligned(2 * strip + which, 8), 128 * j : 128 * j + 128] = src[
                    strip, first : first + 8
                ]
    b_ref[win + 80 : win + 88, :] = jnp.zeros((8, b_ref.shape[1]), f32)
    for j in range(4):
        mine = rest_own_ref[4 * half + j]
        theirs = rest_other_ref[4 * half + j]
        lanes = slice(128 * j, 128 * j + 128)
        b_ref[win : win + 42, lanes] = jnp.where(q == 0, mine, theirs)
        b_ref[win + 42 : win + 84, lanes] = jnp.where(q == 0, theirs, mine)


def first_kernel(own_ref, other_ref, rest_own_ref, rest_other_ref, u_ref, w_ref, b_ref, a_ref):
    q = lax.axis_index("row")
    place_top(q, own_ref, other_ref, [a_ref])
    place_lower(q, 0, own_ref, other_ref, rest_own_ref, rest_other_ref, b_ref)
    factor_loop(a_ref, u_ref, w_ref, b_ref)


def second_kernel(
    own_ref, other_ref, own2_ref, other2_ref, rest_own_ref, rest_other_ref, u1_ref, w1_ref, b1_ref,
    top_out, win_out, rest_out, product_out, l_ref, a_ref, u2_ref, w2_ref, b_ref, sum_ref,
):
    q = lax.axis_index("row")
    c = lax.axis_index("col")
    n_win = win_out.shape[0]
    n_rest = rest_out.shape[0]
    place_top(q, own2_ref, other2_ref, [l_ref, a_ref])
    place_lower(q, 1, own_ref, other_ref, rest_own_ref, rest_other_ref, b_ref)
    solve_rows(l_ref, u1_ref, w1_ref)
    a_ref[...] = a_ref[...] - mm(l_ref[...], l_ref[...], NT)

    def beside():
        b_ref[...] = b_ref[...] - mm(b1_ref[...], l_ref[...], NT)
        sum_ref[...] = mm(b1_ref[n_win:, :], b1_ref[:n_win, :], NT)

    factor_loop(a_ref, u2_ref, w2_ref, b_ref, beside)
    product_out[...] = (sum_ref[...] + mm(b_ref[n_win:, :], b_ref[:n_win, :], NT))[:n_rest]
    left = c < 4

    @pl.when(q == 0)
    def _():
        win_out[...] = b1_ref[:n_win, :]

    @pl.when(q == 1)
    def _():
        win_out[...] = b_ref[:n_win, :]

    @pl.when(left)
    def _():
        rest_out[...] = b1_ref[n_win : n_win + n_rest, aligned(c, 128)]

    @pl.when(jnp.logical_not(left))
    def _():
        rest_out[...] = b_ref[n_win : n_win + n_rest, aligned(c - 4, 128)]

    @pl.when(left & (q == 0))
    def _():
        top_out[...] = u1_ref[aligned(c, 128), :].T

    @pl.when(jnp.logical_not(left) & (q == 0))
    def _():
        top_out[...] = jnp.zeros(top_out.shape, f32)

    @pl.when(left & (q == 1))
    def _():
        top_out[...] = l_ref[:, aligned(c, 128)]

    @pl.when(jnp.logical_not(left) & (q == 1))
    def _():
        top_out[...] = u2_ref[aligned(c - 4, 128), :].T


def call(kernel, outs, scratch, micros, limit, *args, **extra):
    shape = lambda s: jax.ShapeDtypeStruct(s, f32)
    return pl.pallas_call(
        kernel,
        out_shape=tuple(shape(s) for s in outs),
        scratch_shapes=[pltpu.VMEM(s, f32) if isinstance(s, tuple) else s for s in scratch],
        compiler_params=pltpu.CompilerParams(vmem_limit_bytes=limit << 20),
        cost_estimate=pl.CostEstimate(
            flops=int(micros * 1e9), transcendentals=0, bytes_accessed=int(micros * 3e6)
        ),
        **extra,
    )(*args)


def swap_rows(value):
    return lax.ppermute(value, "row", [(0, 1), (1, 0)])


def spread(value, axis):
    n = lax.axis_size(axis)
    return lax.all_to_all(jnp.broadcast_to(value, (n,) + value.shape), axis, 0, 0)


def per_device(panel_top, panel_win, panel_rest, trail_rest):
    q = lax.axis_index("row")
    (pieces,) = call(
        pack_kernel, [(32, 90, 128)], [(1344, 128), pltpu.SemaphoreType.DMA((6,))], 2, 4,
        panel_top[0].reshape(32, 16, 128), panel_win[0].reshape(32, 8, HALF), panel_rest[0],
        in_specs=[pl.BlockSpec(memory_space=pltpu.HBM)] * 3,
    )
    parts = lax.all_to_all(pieces, ("layer", "row"), 0, 0)
    sums = jnp.sum(parts.reshape(16, 2, 90, 128), axis=0)
    sums, trail = lax.optimization_barrier((sums, trail_rest[0].reshape(16, 84, 256)))
    strips = spread(sums[:, 32:], "col")
    own = spread(
        jnp.concatenate([strips[:4, 0, :16].reshape(64, 128), sums[:, :32].reshape(64, 128)], axis=0),
        "layer",
    )
    rest = strips[:, :, 16:]
    rest_own = lax.dynamic_index_in_dim(rest, q, 1, False)
    rest_other = swap_rows(lax.dynamic_index_in_dim(rest, 1 - q, 1, False))
    other = swap_rows(own)
    second = strips[:, 1, :16].reshape(128, 128)
    own, other, second = lax.optimization_barrier((own, other, second))
    own2 = spread(second, "layer")
    u1, w1, b1 = call(
        first_kernel, [(HALF, HALF), (4, 128, 128), (344, HALF)], [(HALF, HALF)], 14, 12,
        own, other, rest_own, rest_other,
    )
    own2, u1, trail = lax.optimization_barrier((own2, u1, trail))
    other2 = swap_rows(own2)
    trail_parts = lax.all_to_all(trail, "layer", 0, 0)
    top_block, win_block, rest_block, product = call(
        second_kernel,
        [(HALF, 128), (256, HALF), (84, 128), (84, 256)],
        [(HALF, HALF), (HALF, HALF), (HALF, HALF), (4, 128, 128), (344, HALF), (88, 256)], 20, 16,
        own, other, own2, other2, rest_own, rest_other, u1, w1, b1,
    )
    return top_block, win_block, rest_block, jnp.sum(trail_parts, axis=0) - product


def solution(mesh):
    return jax.shard_map(
        per_device,
        mesh=mesh,
        in_specs=(
            P("layer", "row", "col"),
            P("layer", "col", "row"),
            P("layer", "row", "col"),
            P("layer", "row", "col"),
        ),
        out_specs=(
            P("row", "col"),
            P("col", "row"),
            P(("row", "layer"), "col"),
            P(("row", "layer"), "col"),
        ),
        check_vma=False,
    )
```

```python
import jax, jax.numpy as jnp
from jax import lax
from jax.sharding import PartitionSpec as P
from jax.experimental import pallas as pl
from jax.experimental.pallas import tpu as pltpu
HALF = 512
f32=jnp.float32; bf16=jnp.bfloat16
NN=(((1,),(0,)),((),())); NT=(((1,),(1,)),((),())); TN=(((0,),(0,)),((),()))

def split(a):
    hi=a.astype(bf16); lo=(a-hi.astype(f32)).astype(bf16)
    return hi,lo

def mm(a,b,dims=NN):
    ah,al=split(a); bh,bl=split(b)
    d=lambda x,y: lax.dot_general(x,y,dims,preferred_element_type=f32)
    return d(ah,bh)+(d(ah,bl)+d(al,bh))

def block_inverse(block):
    lane = lax.broadcasted_iota(jnp.int32, (8, 128), 1)
    sub = lax.broadcasted_iota(jnp.int32, (8, 128), 0)
    wide = lambda x: jnp.broadcast_to(x, (8, 128))
    S = [block[8 * g : 8 * g + 8] for g in range(16)]
    inverse = []
    for t in range(8):
        o = 16 * t
        inside = (lane >= o) & (lane < o + 16)
        mine = (2 * t, 2 * t + 1)
        cols = [[wide(S[g][:, o + j : o + j + 1]) for g in mine] for j in range(16)]
        P = [
            jnp.where(inside, jnp.where(lane - o - 8 * k == sub, 1.0, 0.0), S[g])
            for k, g in enumerate(mine)
        ]
        rows = [jnp.zeros((8, 128), f32)] * 2
        pivots = [jnp.ones((8, 128), f32)] * 2
        for m in range(16):
            k, s = divmod(m, 8)
            here = sub == s
            pivot = wide(cols[m][k][s : s + 1])
            scale = 1.0 / pivot
            pivots[k] = jnp.where(here, pivot, pivots[k])
            rows[k] = jnp.where(here, P[k], rows[k])
            for j in range(m + 1, 16):
                f = wide(cols[j][k][s : s + 1]) * scale
                for i in range(2):
                    x = cols[j][i] - cols[m][i] * f
                    cols[j][i] = jnp.where(here, f, x) if i == k else x
            f = wide(P[k][s : s + 1]) * scale
            for i in range(2):
                x = P[i] - cols[m][i] * f
                P[i] = jnp.where(here, f, x) if i == k else x
        V = [wide(P[m // 8][m % 8 : m % 8 + 1]) for m in range(16)]
        for g in range(2 * t + 2, min(16, 2 * t + 4)):
            x = jnp.where(inside, 0.0, S[g])
            for m in range(16):
                x = x - wide(S[g][:, o + m : o + m + 1]) * V[m]
            S[g] = x
        far = range(2 * t + 4, 16)
        if far:
            pads = [jnp.zeros((n, 128), bf16) for n in (o, 112 - o)]
            full = lambda v: jnp.concatenate(
                [x for x in (pads[0], v, pads[1]) if x.shape[0]], axis=0
            )
            vh, vl = (full(v) for v in split(jnp.concatenate(P, axis=0)))
            xh, xl = split(jnp.concatenate([S[g] for g in far], axis=0))
            d = lambda x, y: lax.dot_general(x, y, NN, preferred_element_type=f32)
            y = d(xh, vh) + (d(xh, vl) + d(xl, vh))
            for n, g in enumerate(far):
                S[g] = jnp.where(inside, 0.0, S[g]) - y[8 * n : 8 * n + 8]
        for k in range(2):
            inverse.append(jnp.where(lane < o + 16, rows[k] * lax.rsqrt(pivots[k]), 0.0))
    return jnp.concatenate(inverse, axis=0)


def factor_loop(a_ref, u_ref, w_ref, b_ref, beside=lambda: None):
    n = a_ref.shape[0]
    blocks = n // 128
    ahead = lax.broadcasted_iota(jnp.int32, (128, n), 1) - lax.broadcasted_iota(
        jnp.int32, (128, n), 0
    )

    def solve(k):
        here = pl.ds(pl.multiple_of(k * 128, 128), 128)
        return here, mm(b_ref[:, here], w_ref[k], NT)

    def step(k, diagonal, first=False):
        o = pl.multiple_of(k * 128, 128)
        inverse = block_inverse(diagonal)
        if first:
            beside()
        else:
            past = u_ref[pl.ds(pl.multiple_of(k * 128 - 128, 128), 128), :]
            a_ref[...] = a_ref[...] - mm(past, past, TN)
            before, solved = solve(k - 1)
            b_ref[...] = b_ref[...] - mm(solved, past)
            b_ref[:, before] = solved
        w_ref[k] = inverse
        panel = mm(inverse, a_ref[pl.ds(o, 128), :])
        u_ref[pl.ds(o, 128), :] = jnp.where(ahead >= o, panel, 0.0)
        following = pl.ds(pl.multiple_of(jnp.minimum(k + 1, blocks - 1) * 128, 128), 128)
        corner = u_ref[pl.ds(o, 128), following]
        return a_ref[following, following] - mm(corner, corner, TN)

    lax.fori_loop(1, blocks, step, step(0, a_ref[0:128, 0:128], True))
    last, solved = solve(blocks - 1)
    b_ref[:, last] = solved


def solve_rows(x_ref, u_ref, w_ref):
    for k in range(x_ref.shape[1] // 128):
        here = slice(128 * k, 128 * k + 128)
        value = x_ref[:, here]
        if k:
            value = value - mm(x_ref[:, : 128 * k], u_ref[0 : 128 * k, here])
        x_ref[:, here] = mm(value, w_ref[k], NT)


def aligned(index, step):
    return pl.ds(pl.multiple_of(index * step, step), step)


def pack_kernel(top_ref, win_ref, rest_ref, out_ref, whole_ref, sems):
    moves = [
        (win_ref.at[:, :, 128 * j : 128 * j + 128], out_ref.at[:, 8 * j : 8 * j + 8])
        for j in range(4)
    ] + [(top_ref, out_ref.at[:, 32:48]), (rest_ref, whole_ref)]
    copies = [pltpu.make_async_copy(*move, sems.at[n]) for n, move in enumerate(moves)]
    for copy in copies[::-1]:
        copy.start()
    for copy in copies[::-1]:
        copy.wait()
    for piece in range(out_ref.shape[0]):
        out_ref[piece, 48:90] = whole_ref[42 * piece : 42 * piece + 42]


def place_top(q, own_ref, other_ref, refs):
    for which, src in ((q, own_ref), (1 - q, other_ref)):
        for strip in range(src.shape[0]):
            for n, dst in enumerate(refs):
                for c in range(4):
                    first = 64 * n + 16 * c
                    dst[aligned(2 * strip + which, 16), 128 * c : 128 * c + 128] = src[
                        strip, first : first + 16
                    ]


def place_lower(q, half, own_ref, other_ref, rest_own_ref, rest_other_ref, b_ref):
    win = 16 * own_ref.shape[0]
    for which, src in ((q, own_ref), (1 - q, other_ref)):
        for strip in range(src.shape[0]):
            for j in range(4):
                first = 64 + 32 * half + 8 * j
                b_ref[aligned(2 * strip + which, 8), 128 * j : 128 * j + 128] = src[
                    strip, first : first + 8
                ]
    b_ref[win + 80 : win + 88, :] = jnp.zeros((8, b_ref.shape[1]), f32)
    for j in range(4):
        mine = rest_own_ref[4 * half + j]
        theirs = rest_other_ref[4 * half + j]
        lanes = slice(128 * j, 128 * j + 128)
        b_ref[win : win + 42, lanes] = jnp.where(q == 0, mine, theirs)
        b_ref[win + 42 : win + 84, lanes] = jnp.where(q == 0, theirs, mine)


def start_all(sources, targets, sems):
    copies = [
        pltpu.make_async_copy(source, target, sems.at[n])
        for n, (source, target) in enumerate(zip(sources, targets))
    ]
    for copy in copies:
        copy.start()
    return copies


def first_kernel(
    own_ref, other_ref, rest_own_ref, rest_other_ref, u_out, w_out, b_out,
    u_ref, w_ref, b_ref, a_ref, sems,
):
    q = lax.axis_index("row")
    place_top(q, own_ref, other_ref, [a_ref])
    place_lower(q, 0, own_ref, other_ref, rest_own_ref, rest_other_ref, b_ref)
    factor_loop(a_ref, u_ref, w_ref, b_ref)
    for copy in start_all((u_ref, w_ref, b_ref), (u_out, w_out, b_out), sems):
        copy.wait()


def second_kernel(
    own_ref, other_ref, own2_ref, other2_ref, rest_own_ref, rest_other_ref, u1_in, w1_in, b1_in,
    top_out, win_out, rest_out, product_out, u1_ref, w1_ref, b1_ref, l_ref, a_ref, u2_ref, w2_ref,
    b_ref, sum_ref, sems,
):
    copies = start_all((u1_in, w1_in, b1_in), (u1_ref, w1_ref, b1_ref), sems)
    q = lax.axis_index("row")
    c = lax.axis_index("col")
    n_win = win_out.shape[0]
    n_rest = rest_out.shape[0]
    place_top(q, own2_ref, other2_ref, [l_ref, a_ref])
    place_lower(q, 1, own_ref, other_ref, rest_own_ref, rest_other_ref, b_ref)
    for copy in copies:
        copy.wait()
    solve_rows(l_ref, u1_ref, w1_ref)
    a_ref[...] = a_ref[...] - mm(l_ref[...], l_ref[...], NT)

    def beside():
        b_ref[...] = b_ref[...] - mm(b1_ref[...], l_ref[...], NT)
        sum_ref[...] = mm(b1_ref[n_win:, :], b1_ref[:n_win, :], NT)

    factor_loop(a_ref, u2_ref, w2_ref, b_ref, beside)
    product_out[...] = (sum_ref[...] + mm(b_ref[n_win:, :], b_ref[:n_win, :], NT))[:n_rest]
    left = c < 4

    @pl.when(q == 0)
    def _():
        win_out[...] = b1_ref[:n_win, :]

    @pl.when(q == 1)
    def _():
        win_out[...] = b_ref[:n_win, :]

    @pl.when(left)
    def _():
        rest_out[...] = b1_ref[n_win : n_win + n_rest, aligned(c, 128)]

    @pl.when(jnp.logical_not(left))
    def _():
        rest_out[...] = b_ref[n_win : n_win + n_rest, aligned(c - 4, 128)]

    @pl.when(left & (q == 0))
    def _():
        top_out[...] = u1_ref[aligned(c, 128), :].T

    @pl.when(jnp.logical_not(left) & (q == 0))
    def _():
        top_out[...] = jnp.zeros(top_out.shape, f32)

    @pl.when(left & (q == 1))
    def _():
        top_out[...] = l_ref[:, aligned(c, 128)]

    @pl.when(jnp.logical_not(left) & (q == 1))
    def _():
        top_out[...] = u2_ref[aligned(c - 4, 128), :].T


def call(kernel, outs, scratch, micros, limit, *args, **extra):
    shape = lambda s: jax.ShapeDtypeStruct(s, f32) if isinstance(s, tuple) else s
    return pl.pallas_call(
        kernel,
        out_shape=tuple(shape(s) for s in outs),
        scratch_shapes=[pltpu.VMEM(s, f32) if isinstance(s, tuple) else s for s in scratch],
        compiler_params=pltpu.CompilerParams(vmem_limit_bytes=limit << 20),
        cost_estimate=pl.CostEstimate(
            flops=int(micros * 1e9), transcendentals=0, bytes_accessed=int(micros * 3e6)
        ),
        **extra,
    )(*args)


def swap_rows(value):
    return lax.ppermute(value, "row", [(0, 1), (1, 0)])


def spread(value, axis):
    n = lax.axis_size(axis)
    return lax.all_to_all(jnp.broadcast_to(value, (n,) + value.shape), axis, 0, 0)


def per_device(panel_top, panel_win, panel_rest, trail_rest):
    q = lax.axis_index("row")
    (pieces,) = call(
        pack_kernel, [(32, 90, 128)], [(1344, 128), pltpu.SemaphoreType.DMA((6,))], 2, 4,
        *(
            pltpu.with_memory_space_constraint(x, pltpu.HBM)
            for x in (
                panel_top[0].reshape(32, 16, 128), panel_win[0].reshape(32, 8, HALF), panel_rest[0]
            )
        ),
        in_specs=[pl.BlockSpec(memory_space=pltpu.HBM)] * 3,
    )
    parts = lax.all_to_all(pieces, ("layer", "row"), 0, 0)
    sums = jnp.sum(parts.reshape(16, 2, 90, 128), axis=0)
    sums, trail = lax.optimization_barrier((sums, trail_rest[0].reshape(16, 84, 256)))
    strips = spread(sums[:, 32:], "col")
    own = spread(
        jnp.concatenate([strips[:4, 0, :16].reshape(64, 128), sums[:, :32].reshape(64, 128)], axis=0),
        "layer",
    )
    rest = strips[:, :, 16:]
    rest_own = lax.dynamic_index_in_dim(rest, q, 1, False)
    rest_other = swap_rows(lax.dynamic_index_in_dim(rest, 1 - q, 1, False))
    other = swap_rows(own)
    second = jnp.broadcast_to(strips[:, 1, :16].reshape(128, 128), (16, 128, 128))
    own, other, second = lax.optimization_barrier((own, other, second))
    own2 = lax.all_to_all(second, "layer", 0, 0)
    carried = [(HALF, HALF), (4, 128, 128), (344, HALF)]
    u1, w1, b1 = call(
        first_kernel, [pltpu.HBM(x, f32) for x in carried],
        carried + [(HALF, HALF), pltpu.SemaphoreType.DMA((3,))], 14, 12,
        own, other, rest_own, rest_other, out_specs=(pl.BlockSpec(memory_space=pltpu.HBM),) * 3,
    )
    u1, w1, b1 = (pltpu.with_memory_space_constraint(x, pltpu.HBM) for x in (u1, w1, b1))
    own2, w1, trail = lax.optimization_barrier((own2, w1, trail))
    other2 = swap_rows(own2)
    trail_parts = lax.all_to_all(trail, "layer", 0, 0)
    top_block, win_block, rest_block, product = call(
        second_kernel,
        [(HALF, 128), (256, HALF), (84, 128), (84, 256)],
        carried
        + [(HALF, HALF), (HALF, HALF), (HALF, HALF), (4, 128, 128), (344, HALF), (88, 256)]
        + [pltpu.SemaphoreType.DMA((3,))],
        20, 20,
        own, other, own2, other2, rest_own, rest_other, u1, w1, b1,
        in_specs=[pl.BlockSpec(memory_space=pltpu.VMEM)] * 6
        + [pl.BlockSpec(memory_space=pltpu.HBM)] * 3,
    )
    schur = trail_parts[0] - product
    for part in range(1, 16):
        schur = schur + trail_parts[part]
    return top_block, win_block, rest_block, schur


def solution(mesh):
    return jax.shard_map(
        per_device,
        mesh=mesh,
        in_specs=(
            P("layer", "row", "col"),
            P("layer", "col", "row"),
            P("layer", "row", "col"),
            P("layer", "row", "col"),
        ),
        out_specs=(
            P("row", "col"),
            P("col", "row"),
            P(("row", "layer"), "col"),
            P(("row", "layer"), "col"),
        ),
        check_vma=False,
    )
```

```python
import jax, jax.numpy as jnp
from jax import lax
from jax.sharding import PartitionSpec as P
from jax.experimental import pallas as pl
from jax.experimental.pallas import tpu as pltpu
HALF = 512
f32=jnp.float32; bf16=jnp.bfloat16
NN=(((1,),(0,)),((),())); NT=(((1,),(1,)),((),())); TN=(((0,),(0,)),((),()))

def split(a):
    hi=a.astype(bf16); lo=(a-hi.astype(f32)).astype(bf16)
    return hi,lo

def mm(a,b,dims=NN):
    ah,al=split(a); bh,bl=split(b)
    d=lambda x,y: lax.dot_general(x,y,dims,preferred_element_type=f32)
    return d(ah,bh)+(d(ah,bl)+d(al,bh))

def block_inverse(block):
    lane = lax.broadcasted_iota(jnp.int32, (8, 128), 1)
    sub = lax.broadcasted_iota(jnp.int32, (8, 128), 0)
    wide = lambda x: jnp.broadcast_to(x, (8, 128))
    S = [block[8 * g : 8 * g + 8] for g in range(16)]
    inverse = []
    for t in range(8):
        o = 16 * t
        inside = (lane >= o) & (lane < o + 16)
        mine = (2 * t, 2 * t + 1)
        cols = [[wide(S[g][:, o + j : o + j + 1]) for g in mine] for j in range(16)]
        P = [
            jnp.where(inside, jnp.where(lane - o - 8 * k == sub, 1.0, 0.0), S[g])
            for k, g in enumerate(mine)
        ]
        rows = [jnp.zeros((8, 128), f32)] * 2
        pivots = [jnp.ones((8, 128), f32)] * 2
        for m in range(16):
            k, s = divmod(m, 8)
            here = sub == s
            pivot = wide(cols[m][k][s : s + 1])
            scale = 1.0 / pivot
            pivots[k] = jnp.where(here, pivot, pivots[k])
            rows[k] = jnp.where(here, P[k], rows[k])
            others = [jnp.where(here, 0.0, cols[m][i]) if i == k else cols[m][i] for i in range(2)]
            for j in range(m + 1, 16):
                f = wide(cols[j][k][s : s + 1]) * scale
                for i in range(2):
                    x = jnp.where(here, f, cols[j][i]) if i == k else cols[j][i]
                    cols[j][i] = x - others[i] * f
            f = wide(P[k][s : s + 1]) * scale
            for i in range(2):
                x = P[i] - cols[m][i] * f
                P[i] = jnp.where(here, f, x) if i == k else x
        V = [wide(P[m // 8][m % 8 : m % 8 + 1]) for m in range(16)]
        for g in range(2 * t + 2, min(16, 2 * t + 4)):
            x = jnp.where(inside, 0.0, S[g])
            parts = [wide(S[g][:, o + m : o + m + 1]) * V[m] for m in range(16)]
            while len(parts) > 4:
                parts = [u + v for u, v in zip(parts[::2], parts[1::2])]
            for part in parts:
                x = x - part
            S[g] = x
        far = range(2 * t + 4, 16)
        if far:
            pads = [jnp.zeros((n, 128), bf16) for n in (o, 112 - o)]
            full = lambda v: jnp.concatenate(
                [x for x in (pads[0], v, pads[1]) if x.shape[0]], axis=0
            )
            vh, vl = (full(v) for v in split(jnp.concatenate(P, axis=0)))
            xh, xl = split(jnp.concatenate([S[g] for g in far], axis=0))
            d = lambda x, y: lax.dot_general(x, y, NN, preferred_element_type=f32)
            y = d(xh, vh) + (d(xh, vl) + d(xl, vh))
            for n, g in enumerate(far):
                S[g] = jnp.where(inside, 0.0, S[g]) - y[8 * n : 8 * n + 8]
        for k in range(2):
            inverse.append(jnp.where(lane < o + 16, rows[k] * lax.rsqrt(pivots[k]), 0.0))
    return jnp.concatenate(inverse, axis=0)


def factor_loop(a_ref, u_ref, w_ref, b_ref, beside=lambda: None):
    n = a_ref.shape[0]
    blocks = n // 128
    ahead = lax.broadcasted_iota(jnp.int32, (128, n), 1) - lax.broadcasted_iota(
        jnp.int32, (128, n), 0
    )

    def solve(k):
        here = pl.ds(pl.multiple_of(k * 128, 128), 128)
        return here, mm(b_ref[:, here], w_ref[k], NT)

    def step(k, diagonal, first=False):
        o = pl.multiple_of(k * 128, 128)
        inverse = block_inverse(diagonal)
        if first:
            beside()
        else:
            past = u_ref[pl.ds(pl.multiple_of(k * 128 - 128, 128), 128), :]
            a_ref[...] = a_ref[...] - mm(past, past, TN)
            before, solved = solve(k - 1)
            b_ref[...] = b_ref[...] - mm(solved, past)
            b_ref[:, before] = solved
        w_ref[k] = inverse
        panel = mm(inverse, a_ref[pl.ds(o, 128), :])
        u_ref[pl.ds(o, 128), :] = jnp.where(ahead >= o, panel, 0.0)
        following = pl.ds(pl.multiple_of(jnp.minimum(k + 1, blocks - 1) * 128, 128), 128)
        corner = u_ref[pl.ds(o, 128), following]
        return a_ref[following, following] - mm(corner, corner, TN)

    lax.fori_loop(1, blocks, step, step(0, a_ref[0:128, 0:128], True))
    last, solved = solve(blocks - 1)
    b_ref[:, last] = solved


def solve_rows(x_ref, u_ref, w_ref):
    for k in range(x_ref.shape[1] // 128):
        here = slice(128 * k, 128 * k + 128)
        value = x_ref[:, here]
        if k:
            value = value - mm(x_ref[:, : 128 * k], u_ref[0 : 128 * k, here])
        x_ref[:, here] = mm(value, w_ref[k], NT)


def aligned(index, step):
    return pl.ds(pl.multiple_of(index * step, step), step)


def pack_kernel(top_ref, win_ref, rest_ref, out_ref, whole_ref, sems):
    moves = [
        (win_ref.at[:, :, 128 * j : 128 * j + 128], out_ref.at[:, 8 * j : 8 * j + 8])
        for j in range(4)
    ] + [(top_ref, out_ref.at[:, 32:48]), (rest_ref, whole_ref)]
    copies = [pltpu.make_async_copy(*move, sems.at[n]) for n, move in enumerate(moves)]
    for copy in copies[::-1]:
        copy.start()
    for copy in copies[::-1]:
        copy.wait()
    for piece in range(out_ref.shape[0]):
        out_ref[piece, 88:96] = jnp.zeros((8, 128), f32)
        out_ref[piece, 48:90] = whole_ref[42 * piece : 42 * piece + 42]


def fan_kernel(strips_ref, out_ref):
    for c in range(8):
        strip = strips_ref[c, 64:80]
        for piece in range(out_ref.shape[0]):
            out_ref[piece, 16 * c : 16 * c + 16] = strip


def place_top(q, own_ref, other_ref, refs):
    for which, src in ((q, own_ref), (1 - q, other_ref)):
        for strip in range(src.shape[0]):
            for n, dst in enumerate(refs):
                for c in range(4):
                    first = 64 * n + 16 * c
                    dst[aligned(2 * strip + which, 16), 128 * c : 128 * c + 128] = src[
                        strip, first : first + 16
                    ]


def place_lower(q, half, own_ref, other_ref, rest_own_ref, rest_other_ref, b_ref):
    win = 16 * own_ref.shape[0]
    for which, src in ((q, own_ref), (1 - q, other_ref)):
        for strip in range(src.shape[0]):
            for j in range(4):
                first = 64 + 32 * half + 8 * j
                b_ref[aligned(2 * strip + which, 8), 128 * j : 128 * j + 128] = src[
                    strip, first : first + 8
                ]
    b_ref[win + 80 : win + 88, :] = jnp.zeros((8, b_ref.shape[1]), f32)
    for j in range(4):
        mine = rest_own_ref[4 * half + j, 0:42]
        theirs = rest_other_ref[4 * half + j, 0:42]
        lanes = slice(128 * j, 128 * j + 128)
        b_ref[win : win + 42, lanes] = jnp.where(q == 0, mine, theirs)
        b_ref[win + 42 : win + 84, lanes] = jnp.where(q == 0, theirs, mine)


def start_all(sources, targets, sems):
    copies = [
        pltpu.make_async_copy(source, target, sems.at[n])
        for n, (source, target) in enumerate(zip(sources, targets))
    ]
    for copy in copies:
        copy.start()
    return copies


def first_kernel(
    own_ref, other_ref, rest_own_ref, rest_other_ref, u_out, w_out, b_out,
    u_ref, w_ref, b_ref, a_ref, sems,
):
    q = lax.axis_index("row")
    place_top(q, own_ref, other_ref, [a_ref])
    place_lower(q, 0, own_ref, other_ref, rest_own_ref, rest_other_ref, b_ref)
    factor_loop(a_ref, u_ref, w_ref, b_ref)
    for copy in start_all((u_ref, w_ref, b_ref), (u_out, w_out, b_out), sems):
        copy.wait()


def second_kernel(
    own_ref, other_ref, own2_ref, other2_ref, rest_own_ref, rest_other_ref, u1_in, w1_in, b1_in,
    top_out, win_out, rest_out, product_out, u1_ref, w1_ref, b1_ref, l_ref, a_ref, u2_ref, w2_ref,
    b_ref, sum_ref, sems,
):
    copies = start_all((u1_in, w1_in, b1_in), (u1_ref, w1_ref, b1_ref), sems)
    q = lax.axis_index("row")
    c = lax.axis_index("col")
    n_win = win_out.shape[0]
    n_rest = rest_out.shape[0]
    place_top(q, own2_ref, other2_ref, [l_ref, a_ref])
    place_lower(q, 1, own_ref, other_ref, rest_own_ref, rest_other_ref, b_ref)
    for copy in copies:
        copy.wait()
    solve_rows(l_ref, u1_ref, w1_ref)
    a_ref[...] = a_ref[...] - mm(l_ref[...], l_ref[...], NT)

    def beside():
        b_ref[...] = b_ref[...] - mm(b1_ref[...], l_ref[...], NT)
        sum_ref[...] = mm(b1_ref[n_win:, :], b1_ref[:n_win, :], NT)

    factor_loop(a_ref, u2_ref, w2_ref, b_ref, beside)
    product_out[...] = (sum_ref[...] + mm(b_ref[n_win:, :], b_ref[:n_win, :], NT))[:n_rest]
    left = c < 4

    @pl.when(q == 0)
    def _():
        win_out[...] = b1_ref[:n_win, :]

    @pl.when(q == 1)
    def _():
        win_out[...] = b_ref[:n_win, :]

    @pl.when(left)
    def _():
        rest_out[...] = b1_ref[n_win : n_win + n_rest, aligned(c, 128)]

    @pl.when(jnp.logical_not(left))
    def _():
        rest_out[...] = b_ref[n_win : n_win + n_rest, aligned(c - 4, 128)]

    @pl.when(left & (q == 0))
    def _():
        top_out[...] = u1_ref[aligned(c, 128), :].T

    @pl.when(jnp.logical_not(left) & (q == 0))
    def _():
        top_out[...] = jnp.zeros(top_out.shape, f32)

    @pl.when(left & (q == 1))
    def _():
        top_out[...] = l_ref[:, aligned(c, 128)]

    @pl.when(jnp.logical_not(left) & (q == 1))
    def _():
        top_out[...] = u2_ref[aligned(c - 4, 128), :].T


def call(kernel, outs, scratch, micros, limit, *args, **extra):
    shape = lambda s: jax.ShapeDtypeStruct(s, f32) if isinstance(s, tuple) else s
    return pl.pallas_call(
        kernel,
        out_shape=tuple(shape(s) for s in outs),
        scratch_shapes=[pltpu.VMEM(s, f32) if isinstance(s, tuple) else s for s in scratch],
        compiler_params=pltpu.CompilerParams(vmem_limit_bytes=limit << 20),
        cost_estimate=pl.CostEstimate(
            flops=int(micros * 1e9), transcendentals=0, bytes_accessed=int(micros * 3e6)
        ),
        **extra,
    )(*args)


def swap_rows(value):
    return lax.ppermute(value, "row", [(0, 1), (1, 0)])


def spread(value, axis):
    n = lax.axis_size(axis)
    return lax.all_to_all(jnp.broadcast_to(value, (n,) + value.shape), axis, 0, 0)


def per_device(panel_top, panel_win, panel_rest, trail_rest):
    q = lax.axis_index("row")
    (pieces,) = call(
        pack_kernel, [(32, 96, 128)], [(1344, 128), pltpu.SemaphoreType.DMA((6,))], 2, 4,
        *(
            pltpu.with_memory_space_constraint(x, pltpu.HBM)
            for x in (
                panel_top[0].reshape(32, 16, 128), panel_win[0].reshape(32, 8, HALF), panel_rest[0]
            )
        ),
        in_specs=[pl.BlockSpec(memory_space=pltpu.HBM)] * 3,
    )
    parts = lax.all_to_all(pieces, ("layer", "row"), 0, 0)
    sums = jnp.sum(parts.reshape(16, 2, 96, 128), axis=0)
    sums, trail = lax.optimization_barrier((sums, trail_rest[0].reshape(16, 84, 256)))
    strips = spread(sums[:, 32:].reshape(128, 128), "col")
    own = spread(
        jnp.concatenate([strips[:4, :16].reshape(64, 128), sums[:, :32].reshape(64, 128)], axis=0),
        "layer",
    )
    rest_own = lax.dynamic_slice_in_dim(strips, 64 * q + 16, 48, 1)
    rest_sent = lax.dynamic_slice_in_dim(strips, 80 - 64 * q, 48, 1)
    (second,) = call(fan_kernel, [(16, 128, 128)], [], 1, 4, strips)
    own, second, rest_own, rest_sent = lax.optimization_barrier((own, second, rest_own, rest_sent))
    other = swap_rows(own)
    rest_other = swap_rows(rest_sent)
    own2 = lax.all_to_all(second, "layer", 0, 0)
    carried = [(HALF, HALF), (4, 128, 128), (344, HALF)]
    u1, w1, b1 = call(
        first_kernel, [pltpu.HBM(x, f32) for x in carried],
        carried + [(HALF, HALF), pltpu.SemaphoreType.DMA((3,))], 14, 12,
        own, other, rest_own, rest_other, out_specs=(pl.BlockSpec(memory_space=pltpu.HBM),) * 3,
    )
    u1, w1, b1 = (pltpu.with_memory_space_constraint(x, pltpu.HBM) for x in (u1, w1, b1))
    own2, w1, trail = lax.optimization_barrier((own2, w1, trail))
    other2 = swap_rows(own2)
    trail_parts = lax.all_to_all(trail, "layer", 0, 0)
    top_block, win_block, rest_block, product = call(
        second_kernel,
        [(HALF, 128), (256, HALF), (84, 128), (84, 256)],
        carried
        + [(HALF, HALF), (HALF, HALF), (HALF, HALF), (4, 128, 128), (344, HALF), (88, 256)]
        + [pltpu.SemaphoreType.DMA((3,))],
        20, 20,
        own, other, own2, other2, rest_own, rest_other, u1, w1, b1,
        in_specs=[pl.BlockSpec(memory_space=pltpu.VMEM)] * 6
        + [pl.BlockSpec(memory_space=pltpu.HBM)] * 3,
    )
    schur = trail_parts[0] - product
    for part in range(1, 16):
        schur = schur + trail_parts[part]
    return top_block, win_block, rest_block, schur


def solution(mesh):
    return jax.shard_map(
        per_device,
        mesh=mesh,
        in_specs=(
            P("layer", "row", "col"),
            P("layer", "col", "row"),
            P("layer", "row", "col"),
            P("layer", "row", "col"),
        ),
        out_specs=(
            P("row", "col"),
            P("col", "row"),
            P(("row", "layer"), "col"),
            P(("row", "layer"), "col"),
        ),
        check_vma=False,
    )
```

```python
import jax, jax.numpy as jnp
from jax import lax
from jax.sharding import PartitionSpec as P
from jax.experimental import pallas as pl
from jax.experimental.pallas import tpu as pltpu
HALF = 512
f32=jnp.float32; bf16=jnp.bfloat16
NN=(((1,),(0,)),((),())); NT=(((1,),(1,)),((),())); TN=(((0,),(0,)),((),()))

def split(a):
    hi=a.astype(bf16); lo=(a-hi.astype(f32)).astype(bf16)
    return hi,lo

def mm(a,b,dims=NN):
    ah,al=split(a); bh,bl=split(b)
    d=lambda x,y: lax.dot_general(x,y,dims,preferred_element_type=f32)
    return d(ah,bh)+(d(ah,bl)+d(al,bh))

def block_inverse(block):
    lane = lax.broadcasted_iota(jnp.int32, (8, 128), 1)
    sub = lax.broadcasted_iota(jnp.int32, (8, 128), 0)
    wide = lambda x: jnp.broadcast_to(x, (8, 128))
    S = [block[8 * g : 8 * g + 8] for g in range(16)]
    inverse = []
    for t in range(8):
        o = 16 * t
        inside = (lane >= o) & (lane < o + 16)
        mine = (2 * t, 2 * t + 1)
        cols = [[wide(S[g][:, o + j : o + j + 1]) for g in mine] for j in range(16)]
        P = [
            jnp.where(inside, jnp.where(lane - o - 8 * k == sub, 1.0, 0.0), S[g])
            for k, g in enumerate(mine)
        ]
        rows = [jnp.zeros((8, 128), f32)] * 2
        pivots = [jnp.ones((8, 128), f32)] * 2
        for m in range(16):
            k, s = divmod(m, 8)
            here = sub == s
            pivot = wide(cols[m][k][s : s + 1])
            scale = 1.0 / pivot
            pivots[k] = jnp.where(here, pivot, pivots[k])
            rows[k] = jnp.where(here, P[k], rows[k])
            others = [jnp.where(here, 0.0, cols[m][i]) if i == k else cols[m][i] for i in range(2)]
            for j in range(m + 1, 16):
                f = wide(cols[j][k][s : s + 1]) * scale
                for i in range(2):
                    x = jnp.where(here, f, cols[j][i]) if i == k else cols[j][i]
                    cols[j][i] = x - others[i] * f
            f = wide(P[k][s : s + 1]) * scale
            for i in range(2):
                x = P[i] - cols[m][i] * f
                P[i] = jnp.where(here, f, x) if i == k else x
        V = [wide(P[m // 8][m % 8 : m % 8 + 1]) for m in range(16)]
        for g in range(2 * t + 2, min(16, 2 * t + 4)):
            x = jnp.where(inside, 0.0, S[g])
            parts = [wide(S[g][:, o + m : o + m + 1]) * V[m] for m in range(16)]
            while len(parts) > 4:
                parts = [u + v for u, v in zip(parts[::2], parts[1::2])]
            for part in parts:
                x = x - part
            S[g] = x
        far = range(2 * t + 4, 16)
        if far:
            pads = [jnp.zeros((n, 128), bf16) for n in (o, 112 - o)]
            full = lambda v: jnp.concatenate(
                [x for x in (pads[0], v, pads[1]) if x.shape[0]], axis=0
            )
            vh, vl = (full(v) for v in split(jnp.concatenate(P, axis=0)))
            xh, xl = split(jnp.concatenate([S[g] for g in far], axis=0))
            d = lambda x, y: lax.dot_general(x, y, NN, preferred_element_type=f32)
            y = d(xh, vh) + (d(xh, vl) + d(xl, vh))
            for n, g in enumerate(far):
                S[g] = jnp.where(inside, 0.0, S[g]) - y[8 * n : 8 * n + 8]
        for k in range(2):
            inverse.append(jnp.where(lane < o + 16, rows[k] * lax.rsqrt(pivots[k]), 0.0))
    return jnp.concatenate(inverse, axis=0)


def factor_loop(a_ref, u_ref, w_ref, b_ref, first_diagonal, beside=lambda: None):
    n = a_ref.shape[0]
    blocks = n // 128
    ahead = lax.broadcasted_iota(jnp.int32, (128, n), 1) - lax.broadcasted_iota(
        jnp.int32, (128, n), 0
    )

    def solve(k):
        here = pl.ds(pl.multiple_of(k * 128, 128), 128)
        return here, mm(b_ref[:, here], w_ref[k], NT)

    def step(k, diagonal, first=False):
        o = pl.multiple_of(k * 128, 128)
        inverse = block_inverse(diagonal)
        if first:
            beside()
        else:
            past = u_ref[pl.ds(pl.multiple_of(k * 128 - 128, 128), 128), :]
            a_ref[...] = a_ref[...] - mm(past, past, TN)
            before, solved = solve(k - 1)
            b_ref[...] = b_ref[...] - mm(solved, past)
            b_ref[:, before] = solved
        w_ref[k] = inverse
        panel = mm(inverse, a_ref[pl.ds(o, 128), :])
        u_ref[pl.ds(o, 128), :] = jnp.where(ahead >= o, panel, 0.0)
        following = pl.ds(pl.multiple_of(jnp.minimum(k + 1, blocks - 1) * 128, 128), 128)
        corner = u_ref[pl.ds(o, 128), following]
        return a_ref[following, following] - mm(corner, corner, TN)

    lax.fori_loop(1, blocks, step, step(0, first_diagonal, True))
    last, solved = solve(blocks - 1)
    b_ref[:, last] = solved


def solve_rows(x_ref, rows, u_ref, w_ref):
    for k in range(x_ref.shape[1] // 128):
        here = slice(128 * k, 128 * k + 128)
        value = x_ref[rows, here]
        if k:
            value = value - mm(x_ref[rows, : 128 * k], u_ref[0 : 128 * k, here])
        x_ref[rows, here] = mm(value, w_ref[k], NT)


def aligned(index, step):
    return pl.ds(pl.multiple_of(index * step, step), step)


def pack_kernel(top_ref, win_ref, rest_ref, out_ref, whole_ref, sems):
    moves = [
        (win_ref.at[:, :, 128 * j : 128 * j + 128], out_ref.at[:, 8 * j : 8 * j + 8])
        for j in range(4)
    ] + [(top_ref, out_ref.at[:, 32:48]), (rest_ref, whole_ref)]
    copies = [pltpu.make_async_copy(*move, sems.at[n]) for n, move in enumerate(moves)]
    for copy in copies[::-1]:
        copy.start()
    for copy in copies[::-1]:
        copy.wait()
    for piece in range(out_ref.shape[0]):
        out_ref[piece, 88:96] = jnp.zeros((8, 128), f32)
        out_ref[piece, 48:90] = whole_ref[42 * piece : 42 * piece + 42]


def fan_kernel(strips_ref, out_ref):
    for c in range(8):
        strip = strips_ref[c, 64:80]
        for piece in range(out_ref.shape[0]):
            out_ref[piece, 16 * c : 16 * c + 16] = strip


def place_top(q, own_ref, other_ref, refs):
    for which, src in ((q, own_ref), (1 - q, other_ref)):
        for strip in range(src.shape[0]):
            for n, dst in enumerate(refs):
                for c in range(4):
                    first = 64 * n + 16 * c
                    dst[aligned(2 * strip + which, 16), 128 * c : 128 * c + 128] = src[
                        strip, first : first + 16
                    ]


def place_lower(q, half, own_ref, other_ref, rest_own_ref, rest_other_ref, b_ref):
    win = 16 * own_ref.shape[0]
    for which, src in ((q, own_ref), (1 - q, other_ref)):
        for strip in range(src.shape[0]):
            for j in range(4):
                first = 64 + 32 * half + 8 * j
                b_ref[aligned(2 * strip + which, 8), 128 * j : 128 * j + 128] = src[
                    strip, first : first + 8
                ]
    b_ref[win + 80 : win + 88, :] = jnp.zeros((8, b_ref.shape[1]), f32)
    for j in range(4):
        mine = rest_own_ref[4 * half + j, 0:42]
        theirs = rest_other_ref[4 * half + j, 0:42]
        lanes = slice(128 * j, 128 * j + 128)
        b_ref[win : win + 42, lanes] = jnp.where(q == 0, mine, theirs)
        b_ref[win + 42 : win + 84, lanes] = jnp.where(q == 0, theirs, mine)


def start_all(sources, targets, sems):
    copies = [
        pltpu.make_async_copy(source, target, sems.at[n])
        for n, (source, target) in enumerate(zip(sources, targets))
    ]
    for copy in copies:
        copy.start()
    return copies


def first_kernel(
    own_ref, other_ref, rest_own_ref, rest_other_ref, u_out, w_out, b_out,
    u_ref, w_ref, b_ref, a_ref, sems,
):
    q = lax.axis_index("row")
    place_top(q, own_ref, other_ref, [a_ref])
    place_lower(q, 0, own_ref, other_ref, rest_own_ref, rest_other_ref, b_ref)
    factor_loop(a_ref, u_ref, w_ref, b_ref, a_ref[0:128, 0:128])
    for copy in start_all((u_ref, w_ref, b_ref), (u_out, w_out, b_out), sems):
        copy.wait()


def second_kernel(
    own_ref, other_ref, own2_ref, other2_ref, rest_own_ref, rest_other_ref, u1_in, w1_in, b1_in,
    top_out, win_out, rest_out, product_out, u1_ref, w1_ref, b1_ref, l_ref, a_ref, u2_ref, w2_ref,
    b_ref, sum_ref, sems,
):
    copies = start_all((u1_in, w1_in, b1_in), (u1_ref, w1_ref, b1_ref), sems)
    q = lax.axis_index("row")
    c = lax.axis_index("col")
    n_win = win_out.shape[0]
    n_rest = rest_out.shape[0]
    place_top(q, own2_ref, other2_ref, [l_ref, a_ref])
    place_lower(q, 1, own_ref, other_ref, rest_own_ref, rest_other_ref, b_ref)
    for copy in copies:
        copy.wait()
    solve_rows(l_ref, slice(0, 128), u1_ref, w1_ref)
    diagonal = a_ref[0:128, 0:128] - mm(l_ref[0:128], l_ref[0:128], NT)

    def beside():
        solve_rows(l_ref, slice(128, HALF), u1_ref, w1_ref)
        a_ref[...] = a_ref[...] - mm(l_ref[...], l_ref[...], NT)
        b_ref[...] = b_ref[...] - mm(b1_ref[...], l_ref[...], NT)
        sum_ref[...] = mm(b1_ref[n_win:, :], b1_ref[:n_win, :], NT)

    factor_loop(a_ref, u2_ref, w2_ref, b_ref, diagonal, beside)
    product_out[...] = (sum_ref[...] + mm(b_ref[n_win:, :], b_ref[:n_win, :], NT))[:n_rest]
    left = c < 4

    @pl.when(q == 0)
    def _():
        win_out[...] = b1_ref[:n_win, :]

    @pl.when(q == 1)
    def _():
        win_out[...] = b_ref[:n_win, :]

    @pl.when(left)
    def _():
        rest_out[...] = b1_ref[n_win : n_win + n_rest, aligned(c, 128)]

    @pl.when(jnp.logical_not(left))
    def _():
        rest_out[...] = b_ref[n_win : n_win + n_rest, aligned(c - 4, 128)]

    @pl.when(left & (q == 0))
    def _():
        top_out[...] = u1_ref[aligned(c, 128), :].T

    @pl.when(jnp.logical_not(left) & (q == 0))
    def _():
        top_out[...] = jnp.zeros(top_out.shape, f32)

    @pl.when(left & (q == 1))
    def _():
        top_out[...] = l_ref[:, aligned(c, 128)]

    @pl.when(jnp.logical_not(left) & (q == 1))
    def _():
        top_out[...] = u2_ref[aligned(c - 4, 128), :].T


def call(kernel, outs, scratch, micros, limit, *args, **extra):
    shape = lambda s: jax.ShapeDtypeStruct(s, f32) if isinstance(s, tuple) else s
    return pl.pallas_call(
        kernel,
        out_shape=tuple(shape(s) for s in outs),
        scratch_shapes=[pltpu.VMEM(s, f32) if isinstance(s, tuple) else s for s in scratch],
        compiler_params=pltpu.CompilerParams(vmem_limit_bytes=limit << 20),
        cost_estimate=pl.CostEstimate(
            flops=int(micros * 1e9), transcendentals=0, bytes_accessed=int(micros * 3e6)
        ),
        **extra,
    )(*args)


def swap_rows(value):
    return lax.ppermute(value, "row", [(0, 1), (1, 0)])


def spread(value, axis):
    n = lax.axis_size(axis)
    return lax.all_to_all(jnp.broadcast_to(value, (n,) + value.shape), axis, 0, 0)


def per_device(panel_top, panel_win, panel_rest, trail_rest):
    q = lax.axis_index("row")
    (pieces,) = call(
        pack_kernel, [(32, 96, 128)], [(1344, 128), pltpu.SemaphoreType.DMA((6,))], 2, 4,
        *(
            pltpu.with_memory_space_constraint(x, pltpu.HBM)
            for x in (
                panel_top[0].reshape(32, 16, 128), panel_win[0].reshape(32, 8, HALF), panel_rest[0]
            )
        ),
        in_specs=[pl.BlockSpec(memory_space=pltpu.HBM)] * 3,
    )
    parts = lax.all_to_all(pieces, ("layer", "row"), 0, 0)
    sums = jnp.sum(parts.reshape(16, 2, 96, 128), axis=0)
    sums, trail = lax.optimization_barrier((sums, trail_rest[0].reshape(16, 84, 256)))
    strips = spread(sums[:, 32:].reshape(128, 128), "col")
    own = spread(
        jnp.concatenate([strips[:4, :16].reshape(64, 128), sums[:, :32].reshape(64, 128)], axis=0),
        "layer",
    )
    rest_own = lax.dynamic_slice_in_dim(strips, 64 * q + 16, 48, 1)
    rest_sent = lax.dynamic_slice_in_dim(strips, 80 - 64 * q, 48, 1)
    (second,) = call(fan_kernel, [(16, 128, 128)], [], 1, 4, strips)
    own, second, rest_own, rest_sent = lax.optimization_barrier((own, second, rest_own, rest_sent))
    other = swap_rows(own)
    rest_other = swap_rows(rest_sent)
    own2 = lax.all_to_all(second, "layer", 0, 0)
    carried = [(HALF, HALF), (4, 128, 128), (344, HALF)]
    u1, w1, b1 = call(
        first_kernel, [pltpu.HBM(x, f32) for x in carried],
        carried + [(HALF, HALF), pltpu.SemaphoreType.DMA((3,))], 14, 12,
        own, other, rest_own, rest_other, out_specs=(pl.BlockSpec(memory_space=pltpu.HBM),) * 3,
    )
    u1, w1, b1 = (pltpu.with_memory_space_constraint(x, pltpu.HBM) for x in (u1, w1, b1))
    own2, w1, trail = lax.optimization_barrier((own2, w1, trail))
    other2 = swap_rows(own2)
    trail_parts = lax.all_to_all(trail, "layer", 0, 0)
    top_block, win_block, rest_block, product = call(
        second_kernel,
        [(HALF, 128), (256, HALF), (84, 128), (84, 256)],
        carried
        + [(HALF, HALF), (HALF, HALF), (HALF, HALF), (4, 128, 128), (344, HALF), (88, 256)]
        + [pltpu.SemaphoreType.DMA((3,))],
        20, 20,
        own, other, own2, other2, rest_own, rest_other, u1, w1, b1,
        in_specs=[pl.BlockSpec(memory_space=pltpu.VMEM)] * 6
        + [pl.BlockSpec(memory_space=pltpu.HBM)] * 3,
    )
    schur = trail_parts[0] - product
    for part in range(1, 16):
        schur = schur + trail_parts[part]
    return top_block, win_block, rest_block, schur


def solution(mesh):
    return jax.shard_map(
        per_device,
        mesh=mesh,
        in_specs=(
            P("layer", "row", "col"),
            P("layer", "col", "row"),
            P("layer", "row", "col"),
            P("layer", "row", "col"),
        ),
        out_specs=(
            P("row", "col"),
            P("col", "row"),
            P(("row", "layer"), "col"),
            P(("row", "layer"), "col"),
        ),
        check_vma=False,
    )
```

```python
import jax, jax.numpy as jnp
from jax import lax
from jax.sharding import PartitionSpec as P
from jax.experimental import pallas as pl
from jax.experimental.pallas import tpu as pltpu
HALF = 512
f32=jnp.float32; bf16=jnp.bfloat16
NN=(((1,),(0,)),((),())); NT=(((1,),(1,)),((),())); TN=(((0,),(0,)),((),()))

def split(a):
    hi=a.astype(bf16); lo=(a-hi.astype(f32)).astype(bf16)
    return hi,lo

def mm(a,b,dims=NN):
    ah,al=split(a); bh,bl=split(b)
    d=lambda x,y: lax.dot_general(x,y,dims,preferred_element_type=f32)
    return d(ah,bh)+(d(ah,bl)+d(al,bh))

def block_inverse(block):
    lane = lax.broadcasted_iota(jnp.int32, (8, 128), 1)
    sub = lax.broadcasted_iota(jnp.int32, (8, 128), 0)
    wide = lambda x: jnp.broadcast_to(x, (8, 128))
    S = [block[8 * g : 8 * g + 8] for g in range(16)]
    inverse = []
    for t in range(8):
        o = 16 * t
        inside = (lane >= o) & (lane < o + 16)
        mine = (2 * t, 2 * t + 1)
        cols = [[wide(S[g][:, o + j : o + j + 1]) for g in mine] for j in range(16)]
        P = [
            jnp.where(inside, jnp.where(lane - o - 8 * k == sub, 1.0, 0.0), S[g])
            for k, g in enumerate(mine)
        ]
        rows = [jnp.zeros((8, 128), f32)] * 2
        pivots = [jnp.ones((8, 128), f32)] * 2
        for m in range(16):
            k, s = divmod(m, 8)
            here = sub == s
            pivot = wide(cols[m][k][s : s + 1])
            scale = 1.0 / pivot
            pivots[k] = jnp.where(here, pivot, pivots[k])
            rows[k] = jnp.where(here, P[k], rows[k])
            others = [jnp.where(here, 0.0, cols[m][i]) if i == k else cols[m][i] for i in range(2)]
            for j in range(m + 1, 16):
                f = wide(cols[j][k][s : s + 1]) * scale
                for i in range(2):
                    x = jnp.where(here, f, cols[j][i]) if i == k else cols[j][i]
                    cols[j][i] = x - others[i] * f
            f = wide(P[k][s : s + 1]) * scale
            for i in range(2):
                x = P[i] - cols[m][i] * f
                P[i] = jnp.where(here, f, x) if i == k else x
        V = [wide(P[m // 8][m % 8 : m % 8 + 1]) for m in range(16)]
        for g in range(2 * t + 2, min(16, 2 * t + 4)):
            x = jnp.where(inside, 0.0, S[g])
            parts = [wide(S[g][:, o + m : o + m + 1]) * V[m] for m in range(16)]
            while len(parts) > 4:
                parts = [u + v for u, v in zip(parts[::2], parts[1::2])]
            for part in parts:
                x = x - part
            S[g] = x
        far = range(2 * t + 4, 16)
        if far:
            pads = [jnp.zeros((n, 128), bf16) for n in (o, 112 - o)]
            full = lambda v: jnp.concatenate(
                [x for x in (pads[0], v, pads[1]) if x.shape[0]], axis=0
            )
            vh, vl = (full(v) for v in split(jnp.concatenate(P, axis=0)))
            xh, xl = split(jnp.concatenate([S[g] for g in far], axis=0))
            d = lambda x, y: lax.dot_general(x, y, NN, preferred_element_type=f32)
            y = d(xh, vh) + (d(xh, vl) + d(xl, vh))
            for n, g in enumerate(far):
                S[g] = jnp.where(inside, 0.0, S[g]) - y[8 * n : 8 * n + 8]
        for k in range(2):
            inverse.append(jnp.where(lane < o + 16, rows[k] * lax.rsqrt(pivots[k]), 0.0))
    return jnp.concatenate(inverse, axis=0)


def factor_loop(a_ref, u_ref, w_ref, b_ref=None, beside=lambda: None):
    n = a_ref.shape[0]
    blocks = n // 128
    ahead = lax.broadcasted_iota(jnp.int32, (128, n), 1) - lax.broadcasted_iota(
        jnp.int32, (128, n), 0
    )

    def solve(k):
        here = pl.ds(pl.multiple_of(k * 128, 128), 128)
        return here, mm(b_ref[:, here], w_ref[k], NT)

    def step(k, diagonal, first=False):
        o = pl.multiple_of(k * 128, 128)
        inverse = block_inverse(diagonal)
        if first:
            beside()
        else:
            past = u_ref[pl.ds(pl.multiple_of(k * 128 - 128, 128), 128), :]
            a_ref[...] = a_ref[...] - mm(past, past, TN)
            if b_ref is not None:
                before, solved = solve(k - 1)
                b_ref[...] = b_ref[...] - mm(solved, past)
                b_ref[:, before] = solved
        w_ref[k] = inverse
        panel = mm(inverse, a_ref[pl.ds(o, 128), :])
        u_ref[pl.ds(o, 128), :] = jnp.where(ahead >= o, panel, 0.0)
        following = pl.ds(pl.multiple_of(jnp.minimum(k + 1, blocks - 1) * 128, 128), 128)
        corner = u_ref[pl.ds(o, 128), following]
        return a_ref[following, following] - mm(corner, corner, TN)

    lax.fori_loop(1, blocks, step, step(0, a_ref[0:128, 0:128], True))
    if b_ref is not None:
        last, solved = solve(blocks - 1)
        b_ref[:, last] = solved


def solve_rows(x_ref, u_ref, w_ref):
    for k in range(x_ref.shape[1] // 128):
        here = slice(128 * k, 128 * k + 128)
        value = x_ref[:, here]
        if k:
            value = value - mm(x_ref[:, : 128 * k], u_ref[0 : 128 * k, here])
        x_ref[:, here] = mm(value, w_ref[k], NT)


def aligned(index, step):
    return pl.ds(pl.multiple_of(index * step, step), step)


def pack_kernel(top_ref, win_ref, rest_ref, out_ref, whole_ref, sems):
    moves = [
        (win_ref.at[:, :, 128 * j : 128 * j + 128], out_ref.at[:, 8 * j : 8 * j + 8])
        for j in range(4)
    ] + [(top_ref, out_ref.at[:, 32:48]), (rest_ref, whole_ref)]
    copies = [pltpu.make_async_copy(*move, sems.at[n]) for n, move in enumerate(moves)]
    for copy in copies[::-1]:
        copy.start()
    for copy in copies[::-1]:
        copy.wait()
    for piece in range(out_ref.shape[0]):
        out_ref[piece, 88:96] = jnp.zeros((8, 128), f32)
        out_ref[piece, 48:90] = whole_ref[42 * piece : 42 * piece + 42]


def fan_kernel(strips_ref, win_ref, out_ref):
    for piece in range(out_ref.shape[0]):
        for half in range(2):
            out_ref[piece, 128 + 32 * half : 160 + 32 * half] = win_ref[half]
    for c in range(8):
        strip = strips_ref[c, 64:80]
        for piece in range(out_ref.shape[0]):
            out_ref[piece, 16 * c : 16 * c + 16] = strip


def place_top(q, own_ref, other_ref, refs):
    for which, src in ((q, own_ref), (1 - q, other_ref)):
        for strip in range(src.shape[0]):
            for n, dst in enumerate(refs):
                for c in range(4):
                    first = 64 * n + 16 * c
                    dst[aligned(2 * strip + which, 16), 128 * c : 128 * c + 128] = src[
                        strip, first : first + 16
                    ]


def place_lower(q, half, own_ref, other_ref, rest_own_ref, rest_other_ref, b_ref):
    win = 16 * own_ref.shape[0]
    for which, src in ((q, own_ref), (1 - q, other_ref)):
        for strip in range(src.shape[0]):
            for j in range(4):
                first = 128 + 32 * half + 8 * j
                b_ref[aligned(2 * strip + which, 8), 128 * j : 128 * j + 128] = src[
                    strip, first : first + 8
                ]
    b_ref[win + 80 : win + 88, :] = jnp.zeros((8, b_ref.shape[1]), f32)
    for j in range(4):
        mine = rest_own_ref[4 * half + j, 0:42]
        theirs = rest_other_ref[4 * half + j, 0:42]
        lanes = slice(128 * j, 128 * j + 128)
        b_ref[win : win + 42, lanes] = jnp.where(q == 0, mine, theirs)
        b_ref[win + 42 : win + 84, lanes] = jnp.where(q == 0, theirs, mine)


def start_all(sources, targets, sems):
    copies = [
        pltpu.make_async_copy(source, target, sems.at[n])
        for n, (source, target) in enumerate(zip(sources, targets))
    ]
    for copy in copies:
        copy.start()
    return copies


def first_kernel(own_ref, other_ref, u_out, w_out, u_ref, w_ref, a_ref, sems):
    q = lax.axis_index("row")
    place_top(q, own_ref, other_ref, [a_ref])
    factor_loop(a_ref, u_ref, w_ref)
    for copy in start_all((u_ref, w_ref), (u_out, w_out), sems):
        copy.wait()


def second_kernel(
    own_ref, other_ref, rest_own_ref, rest_other_ref, u1_in, w1_in,
    top_out, win_out, rest_out, product_out, u1_ref, w1_ref, b1_ref, l_ref, a_ref, u2_ref, w2_ref,
    b_ref, sum_ref, sems,
):
    copies = start_all((u1_in, w1_in), (u1_ref, w1_ref), sems)
    q = lax.axis_index("row")
    c = lax.axis_index("col")
    n_win = win_out.shape[0]
    n_rest = rest_out.shape[0]
    place_top(q, own_ref, other_ref, [l_ref, a_ref])
    for half, dst in enumerate((b1_ref, b_ref)):
        place_lower(q, half, own_ref, other_ref, rest_own_ref, rest_other_ref, dst)
    for copy in copies:
        copy.wait()
    solve_rows(l_ref, u1_ref, w1_ref)
    a_ref[...] = a_ref[...] - mm(l_ref[...], l_ref[...], NT)

    def beside():
        solve_rows(b1_ref, u1_ref, w1_ref)
        b_ref[...] = b_ref[...] - mm(b1_ref[...], l_ref[...], NT)
        sum_ref[...] = mm(b1_ref[n_win:, :], b1_ref[:n_win, :], NT)

    factor_loop(a_ref, u2_ref, w2_ref, b_ref, beside)
    product_out[...] = (sum_ref[...] + mm(b_ref[n_win:, :], b_ref[:n_win, :], NT))[:n_rest]
    left = c < 4

    @pl.when(q == 0)
    def _():
        win_out[...] = b1_ref[:n_win, :]

    @pl.when(q == 1)
    def _():
        win_out[...] = b_ref[:n_win, :]

    @pl.when(left)
    def _():
        rest_out[...] = b1_ref[n_win : n_win + n_rest, aligned(c, 128)]

    @pl.when(jnp.logical_not(left))
    def _():
        rest_out[...] = b_ref[n_win : n_win + n_rest, aligned(c - 4, 128)]

    @pl.when(left & (q == 0))
    def _():
        top_out[...] = u1_ref[aligned(c, 128), :].T

    @pl.when(jnp.logical_not(left) & (q == 0))
    def _():
        top_out[...] = jnp.zeros(top_out.shape, f32)

    @pl.when(left & (q == 1))
    def _():
        top_out[...] = l_ref[:, aligned(c, 128)]

    @pl.when(jnp.logical_not(left) & (q == 1))
    def _():
        top_out[...] = u2_ref[aligned(c - 4, 128), :].T


def call(kernel, outs, scratch, micros, limit, *args, **extra):
    shape = lambda s: jax.ShapeDtypeStruct(s, f32) if isinstance(s, tuple) else s
    return pl.pallas_call(
        kernel,
        out_shape=tuple(shape(s) for s in outs),
        scratch_shapes=[pltpu.VMEM(s, f32) if isinstance(s, tuple) else s for s in scratch],
        compiler_params=pltpu.CompilerParams(vmem_limit_bytes=limit << 20),
        cost_estimate=pl.CostEstimate(
            flops=int(micros * 1e9), transcendentals=0, bytes_accessed=int(micros * 3e6)
        ),
        **extra,
    )(*args)


def swap_rows(value):
    return lax.ppermute(value, "row", [(0, 1), (1, 0)])


def spread(value, axis):
    n = lax.axis_size(axis)
    return lax.all_to_all(jnp.broadcast_to(value, (n,) + value.shape), axis, 0, 0)


def per_device(panel_top, panel_win, panel_rest, trail_rest):
    q = lax.axis_index("row")
    (pieces,) = call(
        pack_kernel, [(32, 96, 128)], [(1344, 128), pltpu.SemaphoreType.DMA((6,))], 2, 4,
        *(
            pltpu.with_memory_space_constraint(x, pltpu.HBM)
            for x in (
                panel_top[0].reshape(32, 16, 128), panel_win[0].reshape(32, 8, HALF), panel_rest[0]
            )
        ),
        in_specs=[pl.BlockSpec(memory_space=pltpu.HBM)] * 3,
    )
    parts = lax.all_to_all(pieces, ("layer", "row"), 0, 0)
    sums = jnp.sum(parts.reshape(16, 2, 96, 128), axis=0)
    sums, trail = lax.optimization_barrier((sums, trail_rest[0].reshape(16, 84, 256)))
    strips = spread(sums[:, 32:].reshape(128, 128), "col")
    own = spread(strips[:4, :16].reshape(64, 128), "layer")
    rest_own = lax.dynamic_slice_in_dim(strips, 64 * q + 16, 48, 1)
    rest_sent = lax.dynamic_slice_in_dim(strips, 80 - 64 * q, 48, 1)
    (second,) = call(fan_kernel, [(16, 192, 128)], [], 1, 6, strips, sums[:, :32])
    own, second, rest_own, rest_sent = lax.optimization_barrier((own, second, rest_own, rest_sent))
    other = swap_rows(own)
    rest_other = swap_rows(rest_sent)
    own2 = lax.all_to_all(second, "layer", 0, 0)
    carried = [(HALF, HALF), (4, 128, 128)]
    u1, w1 = call(
        first_kernel, [pltpu.HBM(x, f32) for x in carried],
        carried + [(HALF, HALF), pltpu.SemaphoreType.DMA((2,))], 14, 12,
        own, other, out_specs=(pl.BlockSpec(memory_space=pltpu.HBM),) * 2,
    )
    u1, w1 = (pltpu.with_memory_space_constraint(x, pltpu.HBM) for x in (u1, w1))
    own2, w1, trail = lax.optimization_barrier((own2, w1, trail))
    other2 = swap_rows(own2)
    trail_parts = lax.all_to_all(trail, "layer", 0, 0)
    top_block, win_block, rest_block, product = call(
        second_kernel,
        [(HALF, 128), (256, HALF), (84, 128), (84, 256)],
        carried
        + [(344, HALF), (HALF, HALF), (HALF, HALF), (HALF, HALF), (4, 128, 128), (344, HALF)]
        + [(88, 256), pltpu.SemaphoreType.DMA((2,))],
        20, 20,
        own2, other2, rest_own, rest_other, u1, w1,
        in_specs=[pl.BlockSpec(memory_space=pltpu.VMEM)] * 4
        + [pl.BlockSpec(memory_space=pltpu.HBM)] * 2,
    )
    schur = trail_parts[0] - product
    for part in range(1, 16):
        schur = schur + trail_parts[part]
    return top_block, win_block, rest_block, schur


def solution(mesh):
    return jax.shard_map(
        per_device,
        mesh=mesh,
        in_specs=(
            P("layer", "row", "col"),
            P("layer", "col", "row"),
            P("layer", "row", "col"),
            P("layer", "row", "col"),
        ),
        out_specs=(
            P("row", "col"),
            P("col", "row"),
            P(("row", "layer"), "col"),
            P(("row", "layer"), "col"),
        ),
        check_vma=False,
    )
```

```python
import jax, jax.numpy as jnp
from jax import lax
from jax.sharding import PartitionSpec as P
from jax.experimental import pallas as pl
from jax.experimental.pallas import tpu as pltpu
HALF = 512
f32=jnp.float32; bf16=jnp.bfloat16
NN=(((1,),(0,)),((),())); NT=(((1,),(1,)),((),())); TN=(((0,),(0,)),((),()))

def split(a):
    hi=a.astype(bf16); lo=(a-hi.astype(f32)).astype(bf16)
    return hi,lo

def mm(a,b,dims=NN):
    ah,al=split(a); bh,bl=split(b)
    d=lambda x,y: lax.dot_general(x,y,dims,preferred_element_type=f32)
    return d(ah,bh)+(d(ah,bl)+d(al,bh))

def block_inverse(block):
    lane = lax.broadcasted_iota(jnp.int32, (8, 128), 1)
    sub = lax.broadcasted_iota(jnp.int32, (8, 128), 0)
    wide = lambda x: jnp.broadcast_to(x, (8, 128))
    S = [block[8 * g : 8 * g + 8] for g in range(16)]
    inverse = []
    for t in range(8):
        o = 16 * t
        inside = (lane >= o) & (lane < o + 16)
        mine = (2 * t, 2 * t + 1)
        cols = [[wide(S[g][:, o + j : o + j + 1]) for g in mine] for j in range(16)]
        P = [
            jnp.where(inside, jnp.where(lane - o - 8 * k == sub, 1.0, 0.0), S[g])
            for k, g in enumerate(mine)
        ]
        rows = [jnp.zeros((8, 128), f32)] * 2
        pivots = [jnp.ones((8, 128), f32)] * 2
        for m in range(16):
            k, s = divmod(m, 8)
            here = sub == s
            pivot = wide(cols[m][k][s : s + 1])
            scale = 1.0 / pivot
            pivots[k] = jnp.where(here, pivot, pivots[k])
            rows[k] = jnp.where(here, P[k], rows[k])
            others = [jnp.where(here, 0.0, cols[m][i]) if i == k else cols[m][i] for i in range(2)]
            for j in range(m + 1, 16):
                f = wide(cols[j][k][s : s + 1]) * scale
                for i in range(2):
                    x = jnp.where(here, f, cols[j][i]) if i == k else cols[j][i]
                    cols[j][i] = x - others[i] * f
            f = wide(P[k][s : s + 1]) * scale
            for i in range(2):
                x = P[i] - cols[m][i] * f
                P[i] = jnp.where(here, f, x) if i == k else x
        V = [wide(P[m // 8][m % 8 : m % 8 + 1]) for m in range(16)]
        for g in range(2 * t + 2, min(16, 2 * t + 4)):
            x = jnp.where(inside, 0.0, S[g])
            parts = [wide(S[g][:, o + m : o + m + 1]) * V[m] for m in range(16)]
            while len(parts) > 4:
                parts = [u + v for u, v in zip(parts[::2], parts[1::2])]
            for part in parts:
                x = x - part
            S[g] = x
        far = range(2 * t + 4, 16)
        if far:
            pads = [jnp.zeros((n, 128), bf16) for n in (o, 112 - o)]
            full = lambda v: jnp.concatenate(
                [x for x in (pads[0], v, pads[1]) if x.shape[0]], axis=0
            )
            vh, vl = (full(v) for v in split(jnp.concatenate(P, axis=0)))
            xh, xl = split(jnp.concatenate([S[g] for g in far], axis=0))
            d = lambda x, y: lax.dot_general(x, y, NN, preferred_element_type=f32)
            y = d(xh, vh) + (d(xh, vl) + d(xl, vh))
            for n, g in enumerate(far):
                S[g] = jnp.where(inside, 0.0, S[g]) - y[8 * n : 8 * n + 8]
        for k in range(2):
            inverse.append(jnp.where(lane < o + 16, rows[k] * lax.rsqrt(pivots[k]), 0.0))
    return jnp.concatenate(inverse, axis=0)


def factor_loop(a_ref, u_ref, w_ref, b_ref, beside=lambda: None):
    n = a_ref.shape[0]
    blocks = n // 128
    ahead = lax.broadcasted_iota(jnp.int32, (128, n), 1) - lax.broadcasted_iota(
        jnp.int32, (128, n), 0
    )

    def solve(k):
        here = pl.ds(pl.multiple_of(k * 128, 128), 128)
        return here, mm(b_ref[:, here], w_ref[k], NT)

    def step(k, diagonal, first=False):
        o = pl.multiple_of(k * 128, 128)
        inverse = block_inverse(diagonal)
        if first:
            beside()
        else:
            past = u_ref[pl.ds(pl.multiple_of(k * 128 - 128, 128), 128), :]
            a_ref[...] = a_ref[...] - mm(past, past, TN)
            before, solved = solve(k - 1)
            b_ref[...] = b_ref[...] - mm(solved, past)
            b_ref[:, before] = solved
        w_ref[k] = inverse
        panel = mm(inverse, a_ref[pl.ds(o, 128), :])
        u_ref[pl.ds(o, 128), :] = jnp.where(ahead >= o, panel, 0.0)
        following = pl.ds(pl.multiple_of(jnp.minimum(k + 1, blocks - 1) * 128, 128), 128)
        corner = u_ref[pl.ds(o, 128), following]
        return a_ref[following, following] - mm(corner, corner, TN)

    lax.fori_loop(1, blocks, step, step(0, a_ref[0:128, 0:128], True))
    last, solved = solve(blocks - 1)
    b_ref[:, last] = solved


def solve_rows(x_ref, u_ref, w_ref):
    for k in range(x_ref.shape[1] // 128):
        here = slice(128 * k, 128 * k + 128)
        value = x_ref[:, here]
        if k:
            value = value - mm(x_ref[:, : 128 * k], u_ref[0 : 128 * k, here])
        x_ref[:, here] = mm(value, w_ref[k], NT)


def aligned(index, step):
    return pl.ds(pl.multiple_of(index * step, step), step)


def pack_kernel(top_ref, win_ref, rest_ref, out_ref, whole_ref, pieces_ref, sems):
    moves = [(rest_ref, whole_ref), (top_ref, out_ref.at[:, 32:48])] + [
        (win_ref.at[:, :, 128 * j : 128 * j + 128], out_ref.at[:, 8 * j : 8 * j + 8])
        for j in range(4)
    ]
    copies = [pltpu.make_async_copy(*move, sems.at[n]) for n, move in enumerate(moves)]
    for copy in copies:
        copy.start()
    copies[0].wait()
    for piece in range(pieces_ref.shape[0]):
        pieces_ref[piece, 40:48] = jnp.zeros((8, 128), f32)
        pieces_ref[piece, 0:42] = whole_ref[42 * piece : 42 * piece + 42]
    last = pltpu.make_async_copy(pieces_ref, out_ref.at[:, 48:96], sems.at[6])
    last.start()
    for copy in copies[1:] + [last]:
        copy.wait()


def finish_kernel(parts_ref, product_ref, out_ref, held_ref, sems):
    n = sems.shape[0]
    each = parts_ref.shape[0] // n
    copies = [
        pltpu.make_async_copy(
            parts_ref.at[each * i : each * i + each], held_ref.at[each * i : each * i + each], sems.at[i]
        )
        for i in range(n)
    ]
    for copy in copies:
        copy.start()
    total = -product_ref[...]
    for i, copy in enumerate(copies):
        copy.wait()
        for part in range(each * i, each * i + each):
            total = total + held_ref[part]
    out_ref[...] = total


def fan_kernel(strips_ref, out_ref):
    for c in range(8):
        strip = strips_ref[c, 64:80]
        for piece in range(out_ref.shape[0]):
            out_ref[piece, 16 * c : 16 * c + 16] = strip


def place_top(q, own_ref, other_ref, refs):
    for which, src in ((q, own_ref), (1 - q, other_ref)):
        for strip in range(src.shape[0]):
            for n, dst in enumerate(refs):
                for c in range(4):
                    first = 64 * n + 16 * c
                    dst[aligned(2 * strip + which, 16), 128 * c : 128 * c + 128] = src[
                        strip, first : first + 16
                    ]


def place_lower(q, half, own_ref, other_ref, rest_own_ref, rest_other_ref, b_ref):
    win = 16 * own_ref.shape[0]
    for which, src in ((q, own_ref), (1 - q, other_ref)):
        for strip in range(src.shape[0]):
            for j in range(4):
                first = 64 + 32 * half + 8 * j
                b_ref[aligned(2 * strip + which, 8), 128 * j : 128 * j + 128] = src[
                    strip, first : first + 8
                ]
    b_ref[win + 80 : win + 88, :] = jnp.zeros((8, b_ref.shape[1]), f32)
    for j in range(4):
        mine = rest_own_ref[4 * half + j, 0:42]
        theirs = rest_other_ref[4 * half + j, 0:42]
        lanes = slice(128 * j, 128 * j + 128)
        b_ref[win : win + 42, lanes] = jnp.where(q == 0, mine, theirs)
        b_ref[win + 42 : win + 84, lanes] = jnp.where(q == 0, theirs, mine)


def start_all(sources, targets, sems):
    copies = [
        pltpu.make_async_copy(source, target, sems.at[n])
        for n, (source, target) in enumerate(zip(sources, targets))
    ]
    for copy in copies:
        copy.start()
    return copies


def first_kernel(
    own_ref, other_ref, rest_own_ref, rest_other_ref, u_out, w_out, b_out,
    u_ref, w_ref, b_ref, a_ref, sems,
):
    q = lax.axis_index("row")
    place_top(q, own_ref, other_ref, [a_ref])
    place_lower(q, 0, own_ref, other_ref, rest_own_ref, rest_other_ref, b_ref)
    factor_loop(a_ref, u_ref, w_ref, b_ref)
    for copy in start_all((u_ref, w_ref, b_ref), (u_out, w_out, b_out), sems):
        copy.wait()


def second_kernel(
    own_ref, other_ref, own2_ref, other2_ref, rest_own_ref, rest_other_ref, u1_in, w1_in, b1_in,
    top_out, win_out, rest_out, product_out, u1_ref, w1_ref, b1_ref, l_ref, a_ref, u2_ref, w2_ref,
    b_ref, sum_ref, sems,
):
    copies = start_all((u1_in, w1_in, b1_in), (u1_ref, w1_ref, b1_ref), sems)
    q = lax.axis_index("row")
    c = lax.axis_index("col")
    n_win = win_out.shape[0]
    n_rest = rest_out.shape[0]
    place_top(q, own2_ref, other2_ref, [l_ref, a_ref])
    place_lower(q, 1, own_ref, other_ref, rest_own_ref, rest_other_ref, b_ref)
    for copy in copies:
        copy.wait()
    solve_rows(l_ref, u1_ref, w1_ref)
    a_ref[...] = a_ref[...] - mm(l_ref[...], l_ref[...], NT)

    def beside():
        b_ref[...] = b_ref[...] - mm(b1_ref[...], l_ref[...], NT)
        sum_ref[...] = mm(b1_ref[n_win:, :], b1_ref[:n_win, :], NT)

    factor_loop(a_ref, u2_ref, w2_ref, b_ref, beside)
    product_out[...] = (sum_ref[...] + mm(b_ref[n_win:, :], b_ref[:n_win, :], NT))[:n_rest]
    left = c < 4

    @pl.when(q == 0)
    def _():
        win_out[...] = b1_ref[:n_win, :]

    @pl.when(q == 1)
    def _():
        win_out[...] = b_ref[:n_win, :]

    @pl.when(left)
    def _():
        rest_out[...] = b1_ref[n_win : n_win + n_rest, aligned(c, 128)]

    @pl.when(jnp.logical_not(left))
    def _():
        rest_out[...] = b_ref[n_win : n_win + n_rest, aligned(c - 4, 128)]

    @pl.when(left & (q == 0))
    def _():
        top_out[...] = u1_ref[aligned(c, 128), :].T

    @pl.when(jnp.logical_not(left) & (q == 0))
    def _():
        top_out[...] = jnp.zeros(top_out.shape, f32)

    @pl.when(left & (q == 1))
    def _():
        top_out[...] = l_ref[:, aligned(c, 128)]

    @pl.when(jnp.logical_not(left) & (q == 1))
    def _():
        top_out[...] = u2_ref[aligned(c - 4, 128), :].T


def call(kernel, outs, scratch, micros, limit, *args, **extra):
    shape = lambda s: jax.ShapeDtypeStruct(s, f32) if isinstance(s, tuple) else s
    return pl.pallas_call(
        kernel,
        out_shape=tuple(shape(s) for s in outs),
        scratch_shapes=[pltpu.VMEM(s, f32) if isinstance(s, tuple) else s for s in scratch],
        compiler_params=pltpu.CompilerParams(vmem_limit_bytes=limit << 20),
        cost_estimate=pl.CostEstimate(
            flops=int(micros * 1e9), transcendentals=0, bytes_accessed=int(micros * 3e6)
        ),
        **extra,
    )(*args)


def swap_rows(value):
    return lax.ppermute(value, "row", [(0, 1), (1, 0)])


def spread(value, axis):
    n = lax.axis_size(axis)
    return lax.all_to_all(jnp.broadcast_to(value, (n,) + value.shape), axis, 0, 0)


def per_device(panel_top, panel_win, panel_rest, trail_rest):
    q = lax.axis_index("row")
    (pieces,) = call(
        pack_kernel, [pltpu.HBM((32, 96, 128), f32)],
        [(1344, 128), (32, 48, 128), pltpu.SemaphoreType.DMA((7,))], 2, 4,
        *(
            pltpu.with_memory_space_constraint(x, pltpu.HBM)
            for x in (
                panel_top[0].reshape(32, 16, 128), panel_win[0].reshape(32, 8, HALF), panel_rest[0]
            )
        ),
        in_specs=[pl.BlockSpec(memory_space=pltpu.HBM)] * 3,
        out_specs=(pl.BlockSpec(memory_space=pltpu.HBM),),
    )
    parts = lax.all_to_all(pieces, ("layer", "row"), 0, 0)
    sums = jnp.sum(parts.reshape(16, 2, 96, 128), axis=0)
    sums, trail = lax.optimization_barrier((sums, trail_rest[0].reshape(16, 84, 256)))
    strips = spread(sums[:, 32:].reshape(128, 128), "col")
    own = spread(
        jnp.concatenate([strips[:4, :16].reshape(64, 128), sums[:, :32].reshape(64, 128)], axis=0),
        "layer",
    )
    rest_own = lax.dynamic_slice_in_dim(strips, 64 * q + 16, 48, 1)
    rest_sent = lax.dynamic_slice_in_dim(strips, 80 - 64 * q, 48, 1)
    (second,) = call(fan_kernel, [(16, 128, 128)], [], 1, 4, strips)
    own, second, rest_own, rest_sent = lax.optimization_barrier((own, second, rest_own, rest_sent))
    other = swap_rows(own)
    rest_other = swap_rows(rest_sent)
    own2 = lax.all_to_all(second, "layer", 0, 0)
    carried = [(HALF, HALF), (4, 128, 128), (344, HALF)]
    u1, w1, b1 = call(
        first_kernel, [pltpu.HBM(x, f32) for x in carried],
        carried + [(HALF, HALF), pltpu.SemaphoreType.DMA((3,))], 14, 12,
        own, other, rest_own, rest_other, out_specs=(pl.BlockSpec(memory_space=pltpu.HBM),) * 3,
    )
    u1, w1, b1 = (pltpu.with_memory_space_constraint(x, pltpu.HBM) for x in (u1, w1, b1))
    own2, w1, trail = lax.optimization_barrier((own2, w1, trail))
    other2 = swap_rows(own2)
    trail_parts = lax.all_to_all(trail, "layer", 0, 0)
    top_block, win_block, rest_block, product = call(
        second_kernel,
        [(HALF, 128), (256, HALF), (84, 128), (84, 256)],
        carried
        + [(HALF, HALF), (HALF, HALF), (HALF, HALF), (4, 128, 128), (344, HALF), (88, 256)]
        + [pltpu.SemaphoreType.DMA((3,))],
        20, 20,
        own, other, own2, other2, rest_own, rest_other, u1, w1, b1,
        in_specs=[pl.BlockSpec(memory_space=pltpu.VMEM)] * 6
        + [pl.BlockSpec(memory_space=pltpu.HBM)] * 3,
    )
    (schur,) = call(
        finish_kernel, [(84, 256)], [(16, 84, 256), pltpu.SemaphoreType.DMA((4,))], 1, 4,
        pltpu.with_memory_space_constraint(trail_parts, pltpu.HBM), product,
        in_specs=[pl.BlockSpec(memory_space=pltpu.HBM), pl.BlockSpec(memory_space=pltpu.VMEM)],
    )
    return top_block, win_block, rest_block, schur


def solution(mesh):
    return jax.shard_map(
        per_device,
        mesh=mesh,
        in_specs=(
            P("layer", "row", "col"),
            P("layer", "col", "row"),
            P("layer", "row", "col"),
            P("layer", "row", "col"),
        ),
        out_specs=(
            P("row", "col"),
            P("col", "row"),
            P(("row", "layer"), "col"),
            P(("row", "layer"), "col"),
        ),
        check_vma=False,
    )
```
